32 devices in a mesh: win: 2 (over y), tm: 4 (over z), row: 2 (over x), col: 2 (over core).
Axes of the slice: x: 2, y: 2, z: 4, core: 2. Of those that a mesh axis runs over, the one named last changes fastest.
Arguments:
- seams: bfloat16 [8, 3, 576, 1920], P(('win', 'tm'), None, 'row', 'col'), parts along dimension 0, may hold values from -24 to 24
- levels: int32 [8, 8, 16], P(('win', 'tm'), 'row', 'col'), parts along dimension 0, may hold values from 0 to 4
- weights: int32 [8], P('win'), parts along dimension 0, may hold values from 16 to 2047
Outputs:
- correction: float32 [8, 3, 576, 1920], P(('win', 'tm'), None, 'row', 'col'), parts along dimension 0
The draws below stay inside these ranges and needn't reach their ends.
There are 2 independent parts, one for each index of `win`. The reference program is written for one: setup_inputs(seed, part) draws one part's arguments, and reference() takes and returns one part's arrays. A program takes and returns all parts, laid end to end along the dimension named above; each array names one. Nothing has to cross between parts.
All inputs are finite; a program needn't handle non-finite values.
Results may differ from the reference program's by a relative error of at most 0.0064.
Values may be sent and summed in bfloat16 or wider, within the bound.
A program may use at most 64 MiB of HBM per device.

```python
import math
import jax
import jax.numpy as jnp
from jax import lax

C = 3
H = 576
W = 1920
GH = 8
GW = 16
FRAMES = 4


def draw_seams(key, part):
    key_base = jax.random.fold_in(key, 11)
    key_noise = jax.random.fold_in(key, 12)
    key_colp = jax.random.fold_in(key, 13)
    key_rowp = jax.random.fold_in(key, 14)
    key_phase = jax.random.fold_in(key, 15)
    col_period = 4 + jax.random.randint(key_colp, (C,), 0, 3)
    row_period = 4 + 2 * jax.random.randint(key_rowp, (C,), 0, 2)
    phases = jax.random.uniform(key_phase, (2, C), jnp.float32, 0.0, 2.0 * math.pi)
    col_ids = jnp.arange(W, dtype=jnp.int32)
    row_ids = jnp.arange(H, dtype=jnp.int32)
    col_frac = (col_ids[None, :] % col_period[:, None]).astype(jnp.float32) / col_period[:, None].astype(jnp.float32)
    row_frac = (row_ids[None, :] % row_period[:, None]).astype(jnp.float32) / row_period[:, None].astype(jnp.float32)
    col_wave = jnp.cos(2.0 * math.pi * col_frac + phases[0][:, None])
    row_wave = jnp.cos(2.0 * math.pi * row_frac + phases[1][:, None])
    base = jax.random.normal(key_base, (C, H, W), jnp.float32) * 0.35
    noise = jax.random.normal(key_noise, (FRAMES, C, H, W), jnp.float32) * 3.0
    stripes = 4.0 * col_wave[:, None, :] + 4.0 * row_wave[:, :, None]
    return jnp.clip(base[None] + stripes[None] + noise, -24.0, 24.0).astype(jnp.bfloat16)


def set_ends(result, key, low, high):
    index_at = [jax.random.randint(jax.random.fold_in(key, axis), (), 0, length) for axis, length in enumerate(result.shape)]
    widest = result.shape.index(max(result.shape))
    beside = index_at[:widest] + [(index_at[widest] + 1) % result.shape[widest]] + index_at[widest + 1:]
    return result.at[tuple(index_at)].set(low).at[tuple(beside)].set(high)


def setup_inputs(seed: int = 0, part: int = 0) -> dict:
    streams_of = jax.random.split(jax.random.key(seed), 4)
    own_keys = jax.random.split(jax.random.fold_in(streams_of[3], part), 4)
    seams = draw_seams(jax.random.fold_in(jax.random.fold_in(streams_of[3], part), 71), part)
    levels = set_ends(jax.random.randint(own_keys[1], (FRAMES, GH, GW), 0, 5), jax.random.fold_in(own_keys[1], 1), 0, 4).astype(jnp.int32)
    weights = set_ends(jax.random.randint(own_keys[2], (FRAMES,), 16, 2048), jax.random.fold_in(own_keys[2], 1), 16, 2047).astype(jnp.int32)
    return dict(seams=seams, levels=levels, weights=weights)


screen = 0.001

def cosine_table(length_all, mode_first, mode_count, cell_first, cell_count):
    mode_ids = mode_first + jnp.arange(mode_count, dtype=jnp.int32)
    cell_ids = cell_first + jnp.arange(cell_count, dtype=jnp.int32)
    phases = (2 * cell_ids[None, :] + 1) * mode_ids[:, None] % (4 * length_all)
    angles = phases.astype(jnp.float32) * (math.pi / (2.0 * length_all))
    scales = jnp.where(mode_ids == 0, math.sqrt(1.0 / length_all), math.sqrt(2.0 / length_all)).astype(jnp.float32)
    return (jnp.cos(angles) * scales[:, None]).astype(jnp.bfloat16)

def laplace_eigen(length_all, mode_first, mode_count):
    mode_ids = (mode_first + jnp.arange(mode_count, dtype=jnp.int32)).astype(jnp.float32)
    sines = jnp.sin(mode_ids * (math.pi / (2.0 * length_all)))
    return 4.0 * sines * sines

def couplings(weights):
    stiff = weights.astype(jnp.float32) / 256.0
    couple = 2.0 * stiff[:-1] * stiff[1:] / (stiff[:-1] + stiff[1:])
    zeroes = jnp.zeros((1,), jnp.float32)
    return (jnp.concatenate([zeroes, couple]), jnp.concatenate([couple, zeroes]))

def reference(seams, levels, weights):
    frames, channels, full_height, full_width = seams.shape
    tile_rows = full_height // levels.shape[1]
    tile_cols = full_width // levels.shape[2]
    tile_level = jnp.repeat(jnp.repeat(levels.astype(jnp.float32) * 0.25, tile_rows, axis=1), tile_cols, axis=2)
    blended = (seams.astype(jnp.float32) * tile_level[:, None]).astype(jnp.bfloat16)
    table_w = cosine_table(full_width, 0, full_width, 0, full_width).astype(jnp.float32)
    table_h = cosine_table(full_height, 0, full_height, 0, full_height).astype(jnp.float32)
    highest = lax.Precision.HIGHEST
    spectrum_w = jnp.einsum('fchw,kw->fchk', blended.astype(jnp.float32), table_w, precision=highest).astype(jnp.bfloat16)
    spectrum = jnp.einsum('qh,fchk->fcqk', table_h, spectrum_w.astype(jnp.float32), precision=highest)
    eigen_sum = laplace_eigen(full_height, 0, full_height)[:, None] + laplace_eigen(full_width, 0, full_width)[None, :]
    couple_below, couple_above = couplings(weights)
    ratio_prev = jnp.zeros((full_height, full_width), jnp.float32)
    value_prev = jnp.zeros((channels, full_height, full_width), jnp.float32)
    reduced_all = []
    ratio_all = []
    for frame in range(frames):
        pivot = screen + eigen_sum + couple_below[frame] + couple_above[frame] - couple_below[frame] * ratio_prev
        value_now = (spectrum[frame] + couple_below[frame] * value_prev) / pivot
        ratio_prev = couple_above[frame] / pivot
        reduced_all.append(value_now)
        ratio_all.append(ratio_prev)
        value_prev = value_now
    solved_all = [None] * frames
    following = jnp.zeros((channels, full_height, full_width), jnp.float32)
    for frame in range(frames - 1, -1, -1):
        following = reduced_all[frame] + ratio_all[frame] * following
        solved_all[frame] = following
    solved = jnp.stack(solved_all).astype(jnp.bfloat16)
    restored = jnp.einsum('qh,fcqk->fchk', table_h, solved.astype(jnp.float32), precision=highest).astype(jnp.bfloat16)
    return jnp.einsum('fchk,kw->fchw', restored.astype(jnp.float32), table_w, precision=highest)
```

```python
import functools
import math

import jax
import jax.numpy as jnp
import ml_dtypes
import numpy as np
from jax import lax
from jax.experimental import pallas as pl
from jax.experimental.pallas import tpu as pltpu
from jax.sharding import PartitionSpec as P

screen = 0.001
LANES = 128
PARTS = 3
HOP = 2
LAG_U = 3
LAG_W = 3
LAG_G = 1
MESH = pl.DeviceIdType.MESH


def cosine_table(length):
    ids = np.arange(length, dtype=np.int64)
    phases = (2 * ids[None, :] + 1) * ids[:, None] % (4 * length)
    angles = phases.astype(np.float32) * np.float32(math.pi / (2.0 * length))
    scales = np.where(ids == 0, math.sqrt(1.0 / length), math.sqrt(2.0 / length)).astype(np.float32)
    table = np.cos(angles.astype(np.float64)).astype(np.float32) * scales[:, None]
    return table.astype(ml_dtypes.bfloat16)


def laplace_eigen(length):
    sines = np.sin(np.arange(length, dtype=np.float32) * np.float32(math.pi / (2.0 * length)))
    return np.float32(4.0) * sines * sines


def kernel(J, R, n, C, M, B, S, seams, levels_in, weights_in, tab_f, tab_b, tab_h, tab_t, eig_r, eig_c, out,
           levels, weights, raw, grid, tf, tb, th, tt, er, ec, x, xg, sw, fr, dd, ee, u, yb, yin, zin, xb, rs, rg,
           i_s, t_s, k_s, g_s, g_r, f_s, f_r, y_s, y_r, z_r, x_s, b_s, b_r, c_s, c_r):
    j, r, t = lax.axis_index("col"), lax.axis_index("row"), lax.axis_index("tm")
    N, D = C * M, J * R
    rows, cols = x.shape[1], x.shape[2]
    H = rows * R
    hs = H // S
    me = j * R + r
    left = t < n // 2
    half = n // 2
    p = jnp.where(left, t, n - 1 - t)
    inner = jnp.where(left, t + 1, t - 1)
    outer = jnp.where(left, t - 1, t + 1)
    mid = p == half - 1

    barrier = pltpu.get_barrier_semaphore()
    for d in range(1, J):
        pl.semaphore_signal(barrier, 1, device_id={"col": lax.rem(j + d, J)}, device_id_type=MESH)
    for d in range(1, R):
        pl.semaphore_signal(barrier, 1, device_id={"row": lax.rem(r + d, R)}, device_id_type=MESH)
    pl.semaphore_signal(barrier, 1, device_id={"tm": inner}, device_id_type=MESH)

    @pl.when(p > 0)
    def _():
        pl.semaphore_signal(barrier, 1, device_id={"tm": outer}, device_id_type=MESH)

    def block(c, m, d):
        return m * D + jnp.where(m == M - 1, lax.rem(d + c, D), d)

    def valid(c, m, d):
        return block(c, m, d) < B

    def slot_of(c, m):
        return jnp.where(m == M - 1, M - 1 + c, m)

    slots = [(0, m) for m in range(M)] + [(c, M - 1) for c in range(1, C)]

    def load(c):
        return pltpu.make_async_copy(seams.at[c], raw.at[c], i_s.at[c])

    def load_table(slot, rr):
        if isinstance(slot, int):
            c, m = slots[slot]
        b = jnp.minimum(block(c, m, j * R + rr), B - 1)
        return pltpu.make_async_copy(tab_f.at[b], tf.at[slot, :, rr * LANES:(rr + 1) * LANES], t_s.at[slot, rr])

    def table_wait(slot, rr):
        return pltpu.make_async_copy(tab_f.at[0], tf.at[slot, :, rr * LANES:(rr + 1) * LANES], t_s.at[slot, rr])

    consts = [pltpu.make_async_copy(s, d, k_s.at[k]) for k, (s, d) in enumerate(
        [(eig_r, er), (eig_c, ec), (tab_h, th), (tab_t, tt), (tab_b.at[j], tb),
         (levels_in, levels), (weights_in, weights)])]

    load(0).start()
    for k in range(5, 7):
        consts[k].start()
    for rr in range(R):
        load_table(0, rr).start()
    for c in range(1, C):
        load(c).start()
    for k in range(2):
        consts[k].start()
    for rr in range(R):
        if len(slots) > 1:
            load_table(1, rr).start()
    consts[2].start()
    for slot in range(2, len(slots)):
        for rr in range(R):
            load_table(slot, rr).start()
    for k in range(3, 5):
        consts[k].start()

    for k in range(5, 7):
        consts[k].wait()
    tile_rows, tile_cols = rows // levels.shape[1], cols // levels.shape[2]
    tile_of = lax.broadcasted_iota(jnp.int32, (1, cols), 1) // tile_cols
    for a in range(levels.shape[1]):
        line = jnp.zeros((1, cols), jnp.float32)
        for b in range(levels.shape[2]):
            line = jnp.where(tile_of == b, levels[0, a, b].astype(jnp.float32) * 0.25, line)
        grid[a * tile_rows:(a + 1) * tile_rows, :] = jnp.broadcast_to(line, (tile_rows, cols))

    stiff = [jnp.full((1, LANES), weights[k].astype(jnp.float32)) * (1.0 / 256.0) for k in range(n)]
    couple = [2.0 * stiff[k] * stiff[k + 1] / (stiff[k] + stiff[k + 1]) for k in range(n - 1)]
    zero = jnp.zeros((1, LANES), jnp.float32)
    ends, flipped = [zero] + couple, [zero] + couple[::-1]
    own = [jnp.where(left, a, b) for a, b in zip(ends, flipped)]
    other = [jnp.where(left, b, a) for a, b in zip(ends, flipped)]
    below, above = own[0], own[1]
    for k in range(1, half):
        below = jnp.where(p == k, own[k], below)
        above = jnp.where(p == k, own[k + 1], above)

    def blend(c):
        load(c).wait()
        x[c] = (raw[c].astype(jnp.float32) * grid[...]).astype(jnp.bfloat16)

    def build_pivots(c, m, slot):
        b = jnp.minimum(block(c, m, me), B - 1)
        a = er[...] + ec[b]

        def sweep(chain):
            rest, first = None, None
            for k in range(half):
                base = a if k == 0 else a + chain[k] * rest
                inverse = 1.0 / (base + chain[k + 1])
                first = inverse if k == 0 else jnp.where(p == k, inverse, first)
                rest = base * inverse
            return base, rest, first

        base, _, first = sweep(own)
        _, rest_other, _ = sweep(other)
        dd[slot] = first
        ee[slot] = jnp.where(p == half - 1, 1.0 / (base + own[half] * rest_other), first)

    def remote(src, dst, ss, rs_, where):
        return pltpu.make_async_remote_copy(
            src_ref=src, dst_ref=dst, send_sem=ss, recv_sem=rs_,
            device_id=where, device_id_type=MESH)

    def lanes_of(c, m, d):
        return pl.ds(pl.multiple_of(jnp.minimum(block(c, m, d), B - 1) * LANES, LANES), LANES)

    def rows_of(rr):
        return pl.ds(pl.multiple_of(rr * rows, 8), rows)

    def q_of(k):
        return pl.ds(pl.multiple_of(k * hs, 16), hs)

    def gather(c, d):
        return remote(x.at[c], xg.at[c, d - 1], g_s.at[c, d - 1], g_r.at[c, d - 1],
                      {"col": lax.rem(j + d, J)})

    def row_out(i, d):
        peer = lax.rem(r + d, R)
        return remote(sw.at[i, peer], fr.at[i, r], f_s.at[i, d - 1], f_r.at[i, d - 1], {"row": peer})

    def y_inner(i, k):
        return remote(yb.at[i, q_of(k)], yin.at[i, q_of(k)], y_s.at[i], y_r.at[i * S + k], {"tm": inner})

    def y_middle(i, k):
        return remote(yb.at[i, q_of(k)], zin.at[i, q_of(k)], y_s.at[i], z_r.at[i * S + k], {"tm": inner})

    def x_outer(i, k):
        return remote(xb.at[i, q_of(k)], zin.at[i, q_of(k)], x_s.at[i], z_r.at[i * S + k], {"tm": outer})

    def row_back(i, c, m, d):
        peer = lax.rem(r + d, R)
        return remote(rs.at[i, peer], rg.at[c, :, lanes_of(c, m, me)], b_s.at[i, d - 1],
                      b_r.at[i, d - 1], {"row": peer})

    def col_share(i, c, m, d, e):
        part = rg.at[c, :, lanes_of(c, m, j * R + lax.rem(r + R - d, R))]
        return remote(part, part, c_s.at[i, d, e - 1], c_r.at[i, d, e - 1],
                      {"col": lax.rem(j + e, J)})

    def whole_wait(ref, sem):
        pltpu.make_async_copy(ref, ref, sem).wait()

    def dot(a, b):
        return jnp.dot(a, b, preferred_element_type=jnp.float32)

    blend(0)

    @pl.when(p > 0)
    def _():
        pl.semaphore_wait(barrier, J + R)

    @pl.when(p == 0)
    def _():
        pl.semaphore_wait(barrier, J + R - 1)

    for c in range(C):
        if c:
            blend(c)
        for d in range(1, J):
            gather(c, d).start()
    for k in range(2):
        consts[k].wait()
    for s, (c, m) in enumerate(slots[:1]):
        build_pivots(c, m, s)

    total = N * S

    def step(s, carry):
        at_u = s - LAG_U

        @pl.when((at_u >= 0) & (at_u < total) & (at_u % S == 0))
        def _():
            i = at_u // S
            c, m = i // M, i % M

            @pl.when(i == 0)
            def _():
                consts[2].wait()

            @pl.when(valid(c, m, me))
            def _():
                for d in range(1, R):
                    row_out(i, d).wait_recv()
                u[i] = dot(th[...], fr[i].reshape(H, LANES))

        at_y = s - LAG_U - HOP * p

        @pl.when((at_y >= 0) & (at_y < total))
        def _():
            i, k = at_y // S, at_y % S
            c, m = i // M, i % M
            slot = slot_of(c, m)
            q = q_of(k)

            @pl.when(valid(c, m, me))
            def _():
                @pl.when(p > 0)
                def _():
                    y_inner(i, k).wait_recv()
                    u[i, q] = u[i, q] + below * yin[i, q].astype(jnp.float32)
                yb[i, q] = (u[i, q] * dd[slot, q]).astype(jnp.bfloat16)

                @pl.when(mid)
                def _():
                    y_middle(i, k).start()

                @pl.when(jnp.logical_not(mid))
                def _():
                    y_inner(i, k).start()

        at_x = s - LAG_U - HOP * (n - 1 - p)

        @pl.when((at_x >= 0) & (at_x < total))
        def _():
            i, k = at_x // S, at_x % S
            c, m = i // M, i % M
            slot = slot_of(c, m)
            q = q_of(k)

            @pl.when(valid(c, m, me))
            def _():
                x_outer(i, k).wait_recv()
                xb[i, q] = ((u[i, q] + above * zin[i, q].astype(jnp.float32)) * ee[slot, q]).astype(jnp.bfloat16)

                @pl.when(p > 0)
                def _():
                    x_outer(i, k).start()

                @pl.when(k == S - 1)
                def _():
                    @pl.when(i == 0)
                    def _():
                        consts[3].wait()
                    back = dot(tt[...], xb[i]).astype(jnp.bfloat16)
                    rs[i] = back.reshape(R, rows, LANES)
                    for d in range(1, R):
                        row_back(i, c, m, d).start()
                    rg[c, :, lanes_of(c, m, me)] = rs[i, r]
                    for e in range(1, J):
                        col_share(i, c, m, 0, e).start()

        at_w = at_x - LAG_W

        @pl.when((at_w >= 0) & (at_w < total) & (at_w % S == S - 1))
        def _():
            i = at_w // S
            c, m = i // M, i % M
            for d in range(1, R):
                @pl.when(valid(c, m, j * R + lax.rem(r + R - d, R)))
                def _():
                    row_back(i, c, m, d).wait_recv()
                    for e in range(1, J):
                        col_share(i, c, m, d, e).start()

        @pl.when((s < total) & (s % S == 0))
        def _():
            i = s // S
            c, m = i // M, i % M
            slot = slot_of(c, m)
            fresh = (c == 0) | (m == M - 1)

            @pl.when(fresh)
            def _():
                for rr in range(R):
                    table_wait(slot, rr).wait()

            @pl.when(m == 0)
            def _():
                for d in range(1, J):
                    gather(c, d).wait_recv()

            def cols_of(d):
                return pl.ds(pl.multiple_of(lax.rem(j + J - d, J) * cols, 16), cols)
            acc = dot(x[c], tf[slot, cols_of(0)])
            for d in range(1, J):
                acc += dot(xg[c, d - 1], tf[slot, cols_of(d)])
            low = acc.astype(jnp.bfloat16)
            for rr in range(R):
                sw[i, rr] = low[:, rr * LANES:(rr + 1) * LANES]
            for d in range(1, R):
                @pl.when(valid(c, m, j * R + lax.rem(r + d, R)))
                def _():
                    row_out(i, d).start()
            fr[i, r] = sw[i, r]

            @pl.when(fresh & (i > 0))
            def _():
                build_pivots(c, m, slot)

        at_g = at_w - LAG_G

        @pl.when((at_g >= 0) & (at_g < total) & (at_g % S == S - 1))
        def _():
            i = at_g // S
            c, m = i // M, i % M

            @pl.when(i == 0)
            def _():
                consts[4].wait()
            for d in range(R):
                for e in range(1, J):
                    @pl.when(valid(c, m, lax.rem(j + J - e, J) * R + lax.rem(r + R - d, R)))
                    def _():
                        col_share(i, c, m, d, e).wait_recv()

            if M > 1:
                @pl.when(m < M - 1)
                def _():
                    span = pl.ds(pl.multiple_of(m * D * LANES, LANES), D * LANES)
                    part = dot(rg[c, :, span], tb[span, :])

                    @pl.when(m == 0)
                    def _():
                        out[c] = part

                    @pl.when(m > 0)
                    def _():
                        out[c] = out[c] + part

            @pl.when(m == M - 1)
            def _():
                first = (M - 1) * D * LANES
                part = dot(rg[c, :, first:], tb[first:, :])
                out[c] = part if M == 1 else out[c] + part

            for d in range(1, R):
                @pl.when(valid(c, m, j * R + lax.rem(r + d, R)))
                def _():
                    row_out(i, d).wait_send()

                @pl.when(valid(c, m, j * R + lax.rem(r + R - d, R)))
                def _():
                    for e in range(1, J):
                        col_share(i, c, m, d, e).wait_send()

            @pl.when(valid(c, m, me))
            def _():
                for d in range(1, R):
                    row_back(i, c, m, d).wait_send()
                for e in range(1, J):
                    col_share(i, c, m, 0, e).wait_send()
                whole_wait(yb.at[i], y_s.at[i])

                @pl.when(p > 0)
                def _():
                    whole_wait(xb.at[i], x_s.at[i])
        return carry

    lax.fori_loop(0, total + LAG_U + HOP * (n - 1) + LAG_W + LAG_G, step, 0)
    for c in range(C):
        for d in range(1, J):
            gather(c, d).wait_send()


def local(seams, levels, weights):
    _, C, rows, cols = seams.shape
    R, J, n = lax.axis_size("row"), lax.axis_size("col"), lax.axis_size("tm")
    H, W = rows * R, cols * J
    D = J * R
    B = W // LANES
    M = -(-B // D)
    N = C * M
    S = PARTS
    Q = M - 1 + C

    table_w, table_h = cosine_table(W), cosine_table(H)
    tab_f = jnp.asarray(np.ascontiguousarray(table_w.reshape(B, LANES, W).transpose(0, 2, 1)))
    tab_b = jnp.asarray(np.ascontiguousarray(table_w.reshape(W, J, cols).transpose(1, 0, 2)))
    tab_h = jnp.asarray(table_h)
    tab_t = jnp.asarray(np.ascontiguousarray(table_h.T))
    eig_r = jnp.asarray(np.ascontiguousarray(
        np.broadcast_to((np.float32(screen) + laplace_eigen(H))[:, None], (H, LANES))))
    eig_c = jnp.asarray(laplace_eigen(W).reshape(B, 1, LANES))

    bf, f32 = jnp.bfloat16, jnp.float32
    vm, dma = pltpu.VMEM, pltpu.SemaphoreType.DMA
    hbm = pl.BlockSpec(memory_space=pltpu.HBM)
    result = pl.pallas_call(
        functools.partial(kernel, J, R, n, C, M, B, S),
        out_shape=pltpu.VMEM((C, rows, cols), f32),
        in_specs=[hbm] * 9,
        out_specs=pl.BlockSpec(memory_space=pltpu.VMEM),
        scratch_shapes=[
            pltpu.SMEM(levels.shape, jnp.int32),
            pltpu.SMEM(weights.shape, jnp.int32),
            vm((C, rows, cols), bf),
            vm((rows, cols), f32),
            vm((Q, W, R * LANES), bf),
            vm((W, cols), bf),
            vm((H, H), bf),
            vm((H, H), bf),
            vm((H, LANES), f32),
            vm((B, 1, LANES), f32),
            vm((C, rows, cols), bf),
            vm((C, J - 1, rows, cols), bf),
            vm((N, R, rows, LANES), bf),
            vm((N, R, rows, LANES), bf),
            vm((Q, H, LANES), f32),
            vm((Q, H, LANES), f32),
            vm((N, H, LANES), f32),
            vm((N, H, LANES), bf),
            vm((N, H, LANES), bf),
            vm((N, H, LANES), bf),
            vm((N, H, LANES), bf),
            vm((N, R, rows, LANES), bf),
            vm((C, rows, W), bf),
            dma((C,)), dma((Q, R)), dma((7,)),
            dma((C, J - 1)), dma((C, J - 1)),
            dma((N, R - 1)), dma((N, R - 1)),
            dma((N,)), dma((N * S,)), dma((N * S,)), dma((N,)),
            dma((N, R - 1)), dma((N, R - 1)),
            dma((N, R, J - 1)), dma((N, R, J - 1)),
        ],
        compiler_params=pltpu.CompilerParams(
            collective_id=0, has_side_effects=True, vmem_limit_bytes=52 * 1024 * 1024),
    )(seams[0], levels, weights, tab_f, tab_b, tab_h, tab_t, eig_r, eig_c)
    return result[None]


def solution(mesh):
    placed = (P(("win", "tm"), None, "row", "col"), P(("win", "tm"), "row", "col"), P("win"))
    return jax.shard_map(
        local,
        mesh=mesh,
        in_specs=placed,
        out_specs=P(("win", "tm"), None, "row", "col"),
        check_vma=False,
    )
```

```python
import functools
import math

import jax
import jax.numpy as jnp
import ml_dtypes
import numpy as np
from jax import lax
from jax.experimental import pallas as pl
from jax.experimental.pallas import tpu as pltpu
from jax.sharding import PartitionSpec as P

screen = 0.001
LANES = 128
PARTS = 3
HOP = 4
STRIDE = 2
LAG_U = 6
LAG_W = 6
LAG_G = 3
MESH = pl.DeviceIdType.MESH


def cosine_table(length):
    ids = np.arange(length, dtype=np.int64)
    phases = (2 * ids[None, :] + 1) * ids[:, None] % (4 * length)
    angles = phases.astype(np.float32) * np.float32(math.pi / (2.0 * length))
    scales = np.where(ids == 0, math.sqrt(1.0 / length), math.sqrt(2.0 / length)).astype(np.float32)
    table = np.cos(angles.astype(np.float64)).astype(np.float32) * scales[:, None]
    return table.astype(ml_dtypes.bfloat16)


def laplace_eigen(length):
    sines = np.sin(np.arange(length, dtype=np.float32) * np.float32(math.pi / (2.0 * length)))
    return np.float32(4.0) * sines * sines


def kernel(J, R, n, C, M, B, S, seams, levels_in, weights_in, tab_f, tab_b, tab_h, tab_t, eig_r, eig_c, out,
           levels, weights, raw, grid, tf, tb, th, tt, er, ec, x, xg, sw, fr, dd, ee, u, yb, yin, zin, xb, rs, rg,
           i_s, t_s, k_s, g_s, g_r, f_s, f_r, y_s, y_r, z_r, x_s, b_s, b_r, c_s, c_r):
    j, r, t = lax.axis_index("col"), lax.axis_index("row"), lax.axis_index("tm")
    N, D = C * M, J * R
    rows, cols = x.shape[1], x.shape[2]
    H = rows * R
    hs = H // S
    me = j * R + r
    left = t < n // 2
    half = n // 2
    p = jnp.where(left, t, n - 1 - t)
    inner = jnp.where(left, t + 1, t - 1)
    outer = jnp.where(left, t - 1, t + 1)
    mid = p == half - 1

    barrier = pltpu.get_barrier_semaphore()
    for d in range(1, J):
        pl.semaphore_signal(barrier, 1, device_id={"col": lax.rem(j + d, J)}, device_id_type=MESH)
    for d in range(1, R):
        pl.semaphore_signal(barrier, 1, device_id={"row": lax.rem(r + d, R)}, device_id_type=MESH)
    pl.semaphore_signal(barrier, 1, device_id={"tm": inner}, device_id_type=MESH)

    @pl.when(p > 0)
    def _():
        pl.semaphore_signal(barrier, 1, device_id={"tm": outer}, device_id_type=MESH)

    def block(c, m, d):
        return m * D + jnp.where(m == M - 1, lax.rem(d + c, D), d)

    def valid(c, m, d):
        return block(c, m, d) < B

    def slot_of(c, m):
        return jnp.where(m == M - 1, M - 1 + c, m)

    slots = [(0, m) for m in range(M)] + [(c, M - 1) for c in range(1, C)]

    def load(c):
        return pltpu.make_async_copy(seams.at[c], raw.at[c], i_s.at[c])

    def load_table(slot, rr):
        if isinstance(slot, int):
            c, m = slots[slot]
        b = jnp.minimum(block(c, m, j * R + rr), B - 1)
        return pltpu.make_async_copy(tab_f.at[b], tf.at[slot, :, rr * LANES:(rr + 1) * LANES], t_s.at[slot, rr])

    def table_wait(slot, rr):
        return pltpu.make_async_copy(tab_f.at[0], tf.at[slot, :, rr * LANES:(rr + 1) * LANES], t_s.at[slot, rr])

    consts = [pltpu.make_async_copy(s, d, k_s.at[k]) for k, (s, d) in enumerate(
        [(eig_r, er), (eig_c, ec), (tab_h, th), (tab_t, tt), (tab_b.at[j], tb),
         (levels_in, levels), (weights_in, weights)])]

    load(0).start()
    for k in range(5, 7):
        consts[k].start()
    for rr in range(R):
        load_table(0, rr).start()

    for k in range(5, 7):
        consts[k].wait()
    tile_rows, tile_cols = rows // levels.shape[1], cols // levels.shape[2]
    tile_of = lax.broadcasted_iota(jnp.int32, (1, cols), 1) // tile_cols
    for a in range(levels.shape[1]):
        line = jnp.zeros((1, cols), jnp.float32)
        for b in range(levels.shape[2]):
            line = jnp.where(tile_of == b, levels[0, a, b].astype(jnp.float32) * 0.25, line)
        grid[a * tile_rows:(a + 1) * tile_rows, :] = jnp.broadcast_to(line, (tile_rows, cols))

    stiff = [jnp.full((1, LANES), weights[k].astype(jnp.float32)) * (1.0 / 256.0) for k in range(n)]
    couple = [2.0 * stiff[k] * stiff[k + 1] / (stiff[k] + stiff[k + 1]) for k in range(n - 1)]
    zero = jnp.zeros((1, LANES), jnp.float32)
    ends, flipped = [zero] + couple, [zero] + couple[::-1]
    own = [jnp.where(left, a, b) for a, b in zip(ends, flipped)]
    other = [jnp.where(left, b, a) for a, b in zip(ends, flipped)]
    below, above = own[0], own[1]
    for k in range(1, half):
        below = jnp.where(p == k, own[k], below)
        above = jnp.where(p == k, own[k + 1], above)

    def blend(c):
        load(c).wait()
        x[c] = (raw[c].astype(jnp.float32) * grid[...]).astype(jnp.bfloat16)

    def build_pivots(c, m, slot):
        b = jnp.minimum(block(c, m, me), B - 1)
        a = er[...] + ec[b]

        def sweep(chain):
            rest, first = None, None
            for k in range(half):
                base = a if k == 0 else a + chain[k] * rest
                inverse = 1.0 / (base + chain[k + 1])
                first = inverse if k == 0 else jnp.where(p == k, inverse, first)
                rest = base * inverse
            return base, rest, first

        base, _, first = sweep(own)
        _, rest_other, _ = sweep(other)
        dd[slot] = first
        ee[slot] = jnp.where(p == half - 1, 1.0 / (base + own[half] * rest_other), first)

    def remote(src, dst, ss, rs_, where):
        return pltpu.make_async_remote_copy(
            src_ref=src, dst_ref=dst, send_sem=ss, recv_sem=rs_,
            device_id=where, device_id_type=MESH)

    def lanes_of(c, m, d):
        return pl.ds(pl.multiple_of(jnp.minimum(block(c, m, d), B - 1) * LANES, LANES), LANES)

    def rows_of(rr):
        return pl.ds(pl.multiple_of(rr * rows, 8), rows)

    def q_of(k):
        return pl.ds(pl.multiple_of(k * hs, 16), hs)

    def gather(c, d):
        return remote(x.at[c], xg.at[c, d - 1], g_s.at[c, d - 1], g_r.at[c, d - 1],
                      {"col": lax.rem(j + d, J)})

    def row_out(i, d):
        peer = lax.rem(r + d, R)
        return remote(sw.at[i, peer], fr.at[i, r], f_s.at[i, d - 1], f_r.at[i, d - 1], {"row": peer})

    def y_inner(i, k):
        return remote(yb.at[i, q_of(k)], yin.at[i, q_of(k)], y_s.at[i], y_r.at[i * S + k], {"tm": inner})

    def y_middle(i, k):
        return remote(yb.at[i, q_of(k)], zin.at[i, q_of(k)], y_s.at[i], z_r.at[i * S + k], {"tm": inner})

    def x_outer(i, k):
        return remote(xb.at[i, q_of(k)], zin.at[i, q_of(k)], x_s.at[i], z_r.at[i * S + k], {"tm": outer})

    def row_back(i, c, m, d):
        peer = lax.rem(r + d, R)
        return remote(rs.at[i, peer], rg.at[c, :, lanes_of(c, m, me)], b_s.at[i, d - 1],
                      b_r.at[i, d - 1], {"row": peer})

    def col_share(i, c, m, d, e):
        part = rg.at[c, :, lanes_of(c, m, j * R + lax.rem(r + R - d, R))]
        return remote(part, part, c_s.at[i, d, e - 1], c_r.at[i, d, e - 1],
                      {"col": lax.rem(j + e, J)})

    def whole_wait(ref, sem):
        pltpu.make_async_copy(ref, ref, sem).wait()

    def dot(a, b):
        return jnp.dot(a, b, preferred_element_type=jnp.float32)

    blend(0)

    @pl.when(p > 0)
    def _():
        pl.semaphore_wait(barrier, J + R)

    @pl.when(p == 0)
    def _():
        pl.semaphore_wait(barrier, J + R - 1)

    for d in range(1, J):
        gather(0, d).start()
    for k in range(2):
        consts[k].start()
    for c in range(1, C):
        load(c).start()
    for slot in range(1, len(slots)):
        for rr in range(R):
            load_table(slot, rr).start()
        if slot == 1:
            consts[2].start()
    for k in range(3, 5):
        consts[k].start()
    for k in range(2):
        consts[k].wait()
    for s, (c, m) in enumerate(slots[:1]):
        build_pivots(c, m, s)

    total = N * S

    def step(s, carry):
        at_u = s - LAG_U

        @pl.when((at_u >= 0) & (at_u < total) & (at_u % S == 0))
        def _():
            i = at_u // S
            c, m = i // M, i % M

            @pl.when(i == 0)
            def _():
                consts[2].wait()

            @pl.when(valid(c, m, me))
            def _():
                for d in range(1, R):
                    row_out(i, d).wait_recv()
                u[i] = dot(th[...], fr[i].reshape(H, LANES))

        at_y = s - LAG_U - HOP * p

        @pl.when((at_y >= 0) & (at_y < total))
        def _():
            i, k = at_y // S, at_y % S
            c, m = i // M, i % M
            slot = slot_of(c, m)
            q = q_of(k)

            @pl.when(valid(c, m, me))
            def _():
                @pl.when(p > 0)
                def _():
                    y_inner(i, k).wait_recv()
                    u[i, q] = u[i, q] + below * yin[i, q].astype(jnp.float32)
                yb[i, q] = (u[i, q] * dd[slot, q]).astype(jnp.bfloat16)

                @pl.when(mid)
                def _():
                    y_middle(i, k).start()

                @pl.when(jnp.logical_not(mid))
                def _():
                    y_inner(i, k).start()

        at_x = s - LAG_U - HOP * (n - 1 - p)

        @pl.when((at_x >= 0) & (at_x < total))
        def _():
            i, k = at_x // S, at_x % S
            c, m = i // M, i % M
            slot = slot_of(c, m)
            q = q_of(k)

            @pl.when(valid(c, m, me))
            def _():
                x_outer(i, k).wait_recv()
                xb[i, q] = ((u[i, q] + above * zin[i, q].astype(jnp.float32)) * ee[slot, q]).astype(jnp.bfloat16)

                @pl.when(p > 0)
                def _():
                    x_outer(i, k).start()

                @pl.when(k == S - 1)
                def _():
                    @pl.when(i == 0)
                    def _():
                        consts[3].wait()
                    back = dot(tt[...], xb[i]).astype(jnp.bfloat16)
                    rs[i] = back.reshape(R, rows, LANES)
                    for d in range(1, R):
                        row_back(i, c, m, d).start()
                    rg[c, :, lanes_of(c, m, me)] = rs[i, r]
                    for e in range(1, J):
                        col_share(i, c, m, 0, e).start()

        at_w = at_x - LAG_W

        @pl.when((at_w >= 0) & (at_w < total) & (at_w % S == S - 1))
        def _():
            i = at_w // S
            c, m = i // M, i % M
            for d in range(1, R):
                @pl.when(valid(c, m, j * R + lax.rem(r + R - d, R)))
                def _():
                    row_back(i, c, m, d).wait_recv()
                    for e in range(1, J):
                        col_share(i, c, m, d, e).start()

        @pl.when((s < N * STRIDE) & (s % STRIDE == 0))
        def _():
            i = s // STRIDE
            c, m = i // M, i % M
            slot = slot_of(c, m)
            fresh = (c == 0) | (m == M - 1)

            @pl.when(fresh)
            def _():
                for rr in range(R):
                    table_wait(slot, rr).wait()

            def cols_of(d):
                return pl.ds(pl.multiple_of(lax.rem(j + J - d, J) * cols, 16), cols)
            first = dot(x[c], tf[slot, cols_of(0)])

            @pl.when(m == 0)
            def _():
                for d in range(1, J):
                    gather(c, d).wait_recv()
            acc = first
            for d in range(1, J):
                acc += dot(xg[c, d - 1], tf[slot, cols_of(d)])
            low = acc.astype(jnp.bfloat16)
            for rr in range(R):
                sw[i, rr] = low[:, rr * LANES:(rr + 1) * LANES]
            for d in range(1, R):
                @pl.when(valid(c, m, j * R + lax.rem(r + d, R)))
                def _():
                    row_out(i, d).start()
            fr[i, r] = sw[i, r]
            for c_next in range(1, C):
                @pl.when(i == c_next - 1)
                def _():
                    blend(c_next)
                    for d in range(1, J):
                        gather(c_next, d).start()

            @pl.when(fresh & (i > 0))
            def _():
                build_pivots(c, m, slot)

        at_g = at_w - LAG_G

        @pl.when((at_g >= 0) & (at_g < total) & (at_g % S == S - 1))
        def _():
            i = at_g // S
            c, m = i // M, i % M

            @pl.when(i == 0)
            def _():
                consts[4].wait()
            for d in range(R):
                for e in range(1, J):
                    @pl.when(valid(c, m, lax.rem(j + J - e, J) * R + lax.rem(r + R - d, R)))
                    def _():
                        col_share(i, c, m, d, e).wait_recv()

            if M > 1:
                @pl.when(m < M - 1)
                def _():
                    span = pl.ds(pl.multiple_of(m * D * LANES, LANES), D * LANES)
                    part = dot(rg[c, :, span], tb[span, :])

                    @pl.when(m == 0)
                    def _():
                        out[c] = part

                    @pl.when(m > 0)
                    def _():
                        out[c] = out[c] + part

            @pl.when(m == M - 1)
            def _():
                first = (M - 1) * D * LANES
                part = dot(rg[c, :, first:], tb[first:, :])
                out[c] = part if M == 1 else out[c] + part

            for d in range(1, R):
                @pl.when(valid(c, m, j * R + lax.rem(r + d, R)))
                def _():
                    row_out(i, d).wait_send()

                @pl.when(valid(c, m, j * R + lax.rem(r + R - d, R)))
                def _():
                    for e in range(1, J):
                        col_share(i, c, m, d, e).wait_send()

            @pl.when(valid(c, m, me))
            def _():
                for d in range(1, R):
                    row_back(i, c, m, d).wait_send()
                for e in range(1, J):
                    col_share(i, c, m, 0, e).wait_send()
                whole_wait(yb.at[i], y_s.at[i])

                @pl.when(p > 0)
                def _():
                    whole_wait(xb.at[i], x_s.at[i])
        return carry

    lax.fori_loop(0, total + LAG_U + HOP * (n - 1) + LAG_W + LAG_G, step, 0)
    for c in range(C):
        for d in range(1, J):
            gather(c, d).wait_send()


def local(seams, levels, weights):
    _, C, rows, cols = seams.shape
    R, J, n = lax.axis_size("row"), lax.axis_size("col"), lax.axis_size("tm")
    H, W = rows * R, cols * J
    D = J * R
    B = W // LANES
    M = -(-B // D)
    N = C * M
    S = PARTS
    Q = M - 1 + C

    table_w, table_h = cosine_table(W), cosine_table(H)
    tab_f = jnp.asarray(np.ascontiguousarray(table_w.reshape(B, LANES, W).transpose(0, 2, 1)))
    tab_b = jnp.asarray(np.ascontiguousarray(table_w.reshape(W, J, cols).transpose(1, 0, 2)))
    tab_h = jnp.asarray(table_h)
    tab_t = jnp.asarray(np.ascontiguousarray(table_h.T))
    eig_r = jnp.asarray(np.ascontiguousarray(
        np.broadcast_to((np.float32(screen) + laplace_eigen(H))[:, None], (H, LANES))))
    eig_c = jnp.asarray(laplace_eigen(W).reshape(B, 1, LANES))

    bf, f32 = jnp.bfloat16, jnp.float32
    vm, dma = pltpu.VMEM, pltpu.SemaphoreType.DMA
    hbm = pl.BlockSpec(memory_space=pltpu.HBM)
    result = pl.pallas_call(
        functools.partial(kernel, J, R, n, C, M, B, S),
        out_shape=pltpu.VMEM((C, rows, cols), f32),
        in_specs=[hbm] * 9,
        out_specs=pl.BlockSpec(memory_space=pltpu.VMEM),
        scratch_shapes=[
            pltpu.SMEM(levels.shape, jnp.int32),
            pltpu.SMEM(weights.shape, jnp.int32),
            vm((C, rows, cols), bf),
            vm((rows, cols), f32),
            vm((Q, W, R * LANES), bf),
            vm((W, cols), bf),
            vm((H, H), bf),
            vm((H, H), bf),
            vm((H, LANES), f32),
            vm((B, 1, LANES), f32),
            vm((C, rows, cols), bf),
            vm((C, J - 1, rows, cols), bf),
            vm((N, R, rows, LANES), bf),
            vm((N, R, rows, LANES), bf),
            vm((Q, H, LANES), f32),
            vm((Q, H, LANES), f32),
            vm((N, H, LANES), f32),
            vm((N, H, LANES), bf),
            vm((N, H, LANES), bf),
            vm((N, H, LANES), bf),
            vm((N, H, LANES), bf),
            vm((N, R, rows, LANES), bf),
            vm((C, rows, W), bf),
            dma((C,)), dma((Q, R)), dma((7,)),
            dma((C, J - 1)), dma((C, J - 1)),
            dma((N, R - 1)), dma((N, R - 1)),
            dma((N,)), dma((N * S,)), dma((N * S,)), dma((N,)),
            dma((N, R - 1)), dma((N, R - 1)),
            dma((N, R, J - 1)), dma((N, R, J - 1)),
        ],
        compiler_params=pltpu.CompilerParams(
            collective_id=0, has_side_effects=True, vmem_limit_bytes=52 * 1024 * 1024),
    )(seams[0], levels, weights, tab_f, tab_b, tab_h, tab_t, eig_r, eig_c)
    return result[None]


def solution(mesh):
    placed = (P(("win", "tm"), None, "row", "col"), P(("win", "tm"), "row", "col"), P("win"))
    return jax.shard_map(
        local,
        mesh=mesh,
        in_specs=placed,
        out_specs=P(("win", "tm"), None, "row", "col"),
        check_vma=False,
    )
```

```python
import functools
import math

import jax
import jax.numpy as jnp
import ml_dtypes
import numpy as np
from jax import lax
from jax.experimental import pallas as pl
from jax.experimental.pallas import tpu as pltpu
from jax.sharding import PartitionSpec as P

screen = 0.001
LANES = 128
PARTS = 3
HOP_UP = 4
HOP_MID = 4
HOP_DOWN = 3
FAST = 2
STRIDE = 2
LAG_U = 5
LAG_W = 6
LAG_G = 3
MESH = pl.DeviceIdType.MESH


def cosine_table(length):
    ids = np.arange(length, dtype=np.int64)
    phases = (2 * ids[None, :] + 1) * ids[:, None] % (4 * length)
    angles = phases.astype(np.float32) * np.float32(math.pi / (2.0 * length))
    scales = np.where(ids == 0, math.sqrt(1.0 / length), math.sqrt(2.0 / length)).astype(np.float32)
    table = np.cos(angles.astype(np.float64)).astype(np.float32) * scales[:, None]
    return table.astype(ml_dtypes.bfloat16)


def laplace_eigen(length):
    sines = np.sin(np.arange(length, dtype=np.float32) * np.float32(math.pi / (2.0 * length)))
    return np.float32(4.0) * sines * sines


def kernel(J, R, n, C, M, B, S, seams, levels_in, weights_in, tab_f, tab_b, tab_h, tab_t, tab_p, eig_r, eig_c, out,
           levels, weights, raw, grid, tf, tb, th, tt, tp, ys, yd, er, ec, x, xg, sw, fr, dd, ee, u, yb, yin, zin, xb, rs, rg,
           i_s, t_s, k_s, g_s, g_r, f_s, f_r, y_s, y_r, z_r, x_s, b_s, b_r, c_s, c_r, e_s, e_r):
    j, r, t = lax.axis_index("col"), lax.axis_index("row"), lax.axis_index("tm")
    N, D = C * M, J * R
    rows, cols = x.shape[1], x.shape[2]
    H = rows * R
    hs = H // S
    me = j * R + r
    left = t < n // 2
    half = n // 2
    p = jnp.where(left, t, n - 1 - t)
    inner = jnp.where(left, t + 1, t - 1)
    outer = jnp.where(left, t - 1, t + 1)
    mid = p == half - 1

    barrier = pltpu.get_barrier_semaphore()
    for d in range(1, J):
        pl.semaphore_signal(barrier, 1, device_id={"col": lax.rem(j + d, J)}, device_id_type=MESH)
    for d in range(1, R):
        pl.semaphore_signal(barrier, 1, device_id={"row": lax.rem(r + d, R)}, device_id_type=MESH)
    pl.semaphore_signal(barrier, 1, device_id={"tm": inner}, device_id_type=MESH)

    for d in range(1, R):
        pl.semaphore_signal(barrier, 1, device_id={"tm": inner, "row": lax.rem(r + d, R)}, device_id_type=MESH)

    @pl.when(p > 0)
    def _():
        pl.semaphore_signal(barrier, 1, device_id={"tm": outer}, device_id_type=MESH)
        for d in range(1, R):
            pl.semaphore_signal(barrier, 1, device_id={"tm": outer, "row": lax.rem(r + d, R)}, device_id_type=MESH)

    def block(c, m, d):
        return m * D + jnp.where(m == M - 1, lax.rem(d + c, D), d)

    def valid(c, m, d):
        return block(c, m, d) < B

    def slot_of(c, m):
        return jnp.where(m == M - 1, M - 1 + c, m)

    slots = [(0, m) for m in range(M)] + [(c, M - 1) for c in range(1, C)]

    def load(c):
        return pltpu.make_async_copy(seams.at[c], raw.at[c], i_s.at[c])

    def load_table(slot, rr):
        if isinstance(slot, int):
            c, m = slots[slot]
        b = jnp.minimum(block(c, m, j * R + rr), B - 1)
        return pltpu.make_async_copy(tab_f.at[b], tf.at[slot, :, rr * LANES:(rr + 1) * LANES], t_s.at[slot, rr])

    def table_wait(slot, rr):
        return pltpu.make_async_copy(tab_f.at[0], tf.at[slot, :, rr * LANES:(rr + 1) * LANES], t_s.at[slot, rr])

    consts = [pltpu.make_async_copy(s, d, k_s.at[k]) for k, (s, d) in enumerate(
        [(eig_r, er), (eig_c, ec), (tab_h, th), (tab_t, tt), (tab_b.at[j], tb),
         (levels_in, levels), (weights_in, weights)])]
    fast = min(FAST, S) if half > 1 else 0
    ahead = fast * hs
    if fast:
        early = pltpu.make_async_copy(tab_p.at[r, pl.ds(0, ahead)], tp, k_s.at[7])

    load(0).start()
    for k in range(5, 7):
        consts[k].start()
    for rr in range(R):
        load_table(0, rr).start()
    for k in range(2):
        consts[k].start()
    if fast:
        early.start()

    for k in range(5, 7):
        consts[k].wait()
    tile_rows, tile_cols = rows // levels.shape[1], cols // levels.shape[2]
    tile_of = lax.broadcasted_iota(jnp.int32, (1, cols), 1) // tile_cols
    for a in range(levels.shape[1]):
        line = jnp.zeros((1, cols), jnp.float32)
        for b in range(levels.shape[2]):
            line = jnp.where(tile_of == b, levels[0, a, b].astype(jnp.float32) * 0.25, line)
        grid[a * tile_rows:(a + 1) * tile_rows, :] = jnp.broadcast_to(line, (tile_rows, cols))

    stiff = [jnp.full((1, LANES), weights[k].astype(jnp.float32)) * (1.0 / 256.0) for k in range(n)]
    couple = [2.0 * stiff[k] * stiff[k + 1] / (stiff[k] + stiff[k + 1]) for k in range(n - 1)]
    zero = jnp.zeros((1, LANES), jnp.float32)
    ends, flipped = [zero] + couple, [zero] + couple[::-1]
    own = [jnp.where(left, a, b) for a, b in zip(ends, flipped)]
    other = [jnp.where(left, b, a) for a, b in zip(ends, flipped)]
    below, above = own[0], own[1]
    for k in range(1, half):
        below = jnp.where(p == k, own[k], below)
        above = jnp.where(p == k, own[k + 1], above)

    def blend(c):
        load(c).wait()
        x[c] = (raw[c].astype(jnp.float32) * grid[...]).astype(jnp.bfloat16)

    def build_pivots(c, m, slot):
        b = jnp.minimum(block(c, m, me), B - 1)
        a = er[...] + ec[b]

        def sweep(chain):
            rest, first = None, None
            for k in range(half):
                base = a if k == 0 else a + chain[k] * rest
                inverse = 1.0 / (base + chain[k + 1])
                first = inverse if k == 0 else jnp.where(p == k, inverse, first)
                rest = base * inverse
            return base, rest, first

        base, _, first = sweep(own)
        _, rest_other, _ = sweep(other)
        dd[slot] = first
        ee[slot] = jnp.where(p == half - 1, 1.0 / (base + own[half] * rest_other), first)

    def remote(src, dst, ss, rs_, where):
        return pltpu.make_async_remote_copy(
            src_ref=src, dst_ref=dst, send_sem=ss, recv_sem=rs_,
            device_id=where, device_id_type=MESH)

    def lanes_of(c, m, d):
        return pl.ds(pl.multiple_of(jnp.minimum(block(c, m, d), B - 1) * LANES, LANES), LANES)

    def q_of(k):
        return pl.ds(pl.multiple_of(k * hs, 16), hs)

    def gather(c, d):
        return remote(x.at[c], xg.at[c, d - 1], g_s.at[c, d - 1], g_r.at[c, d - 1],
                      {"col": lax.rem(j + d, J)})

    def row_out(i, d):
        peer = lax.rem(r + d, R)
        return remote(sw.at[i, peer], fr.at[i, r], f_s.at[i, d - 1], f_r.at[i, d - 1], {"row": peer})

    def y_inner(i, k):
        return remote(yb.at[i, q_of(k)], yin.at[i, q_of(k)], y_s.at[i], y_r.at[i * S + k], {"tm": inner})

    def y_early(d, k):
        peer = lax.rem(r + d, R)
        return remote(ys.at[peer, q_of(k)], yd.at[d, q_of(k)], e_s.at[d, k], e_r.at[d, k],
                      {"tm": inner, "row": peer})

    def y_middle(i, k):
        return remote(yb.at[i, q_of(k)], zin.at[i, q_of(k)], y_s.at[i], z_r.at[i * S + k], {"tm": inner})

    def x_outer(i, k):
        return remote(xb.at[i, q_of(k)], zin.at[i, q_of(k)], x_s.at[i], z_r.at[i * S + k], {"tm": outer})

    def row_back(i, c, m, d):
        peer = lax.rem(r + d, R)
        return remote(rs.at[i, peer], rg.at[c, :, lanes_of(c, m, me)], b_s.at[i, d - 1],
                      b_r.at[i, d - 1], {"row": peer})

    def col_share(i, c, m, d, e):
        part = rg.at[c, :, lanes_of(c, m, j * R + lax.rem(r + R - d, R))]
        return remote(part, part, c_s.at[i, d, e - 1], c_r.at[i, d, e - 1],
                      {"col": lax.rem(j + e, J)})

    def whole_wait(ref, sem):
        pltpu.make_async_copy(ref, ref, sem).wait()

    def dot(a, b):
        return jnp.dot(a, b, preferred_element_type=jnp.float32)

    blend(0)

    @pl.when(p > 0)
    def _():
        pl.semaphore_wait(barrier, J + R + 2 * (R - 1))

    @pl.when(p == 0)
    def _():
        pl.semaphore_wait(barrier, J + R - 1 + R - 1)

    for d in range(1, J):
        gather(0, d).start()
    for c in range(1, C):
        load(c).start()
    for slot in range(1, len(slots)):
        for rr in range(R):
            load_table(slot, rr).start()
        if slot == 1:
            consts[2].start()
    for k in range(3, 5):
        consts[k].start()
    for k in range(2):
        consts[k].wait()
    build_pivots(0, 0, 0 if M > 1 else M - 1)

    total = N * S

    def step(s, carry):
        at_u = s - LAG_U - HOP_UP * p
        at_y = at_u - 1
        at_x = s - LAG_U - 1 - HOP_UP * (half - 1) - HOP_MID - HOP_DOWN * (half - 1 - p)
        at_w = at_x - LAG_W
        at_g = at_w - LAG_G

        @pl.when((at_x >= 0) & (at_x < total))
        def _():
            i, k = at_x // S, at_x % S
            c, m = i // M, i % M
            slot = slot_of(c, m)
            q = q_of(k)

            @pl.when(valid(c, m, me))
            def _():
                x_outer(i, k).wait_recv()
                xb[i, q] = ((u[i, q] + above * zin[i, q].astype(jnp.float32)) * ee[slot, q]).astype(jnp.bfloat16)

                @pl.when(p > 0)
                def _():
                    x_outer(i, k).start()

                @pl.when(k == S - 1)
                def _():
                    @pl.when(i == 0)
                    def _():
                        consts[3].wait()
                    for d in range(1, R):
                        peer = lax.rem(r + d, R)
                        rs[i, peer] = dot(tt[peer], xb[i]).astype(jnp.bfloat16)
                        row_back(i, c, m, d).start()
                    rg[c, :, lanes_of(c, m, me)] = dot(tt[r], xb[i]).astype(jnp.bfloat16)
                    for e in range(1, J):
                        col_share(i, c, m, 0, e).start()

        @pl.when((at_y >= 0) & (at_y < total))
        def _():
            i, k = at_y // S, at_y % S
            c, m = i // M, i % M
            slot = slot_of(c, m)
            q = q_of(k)

            is_early = (i == 0) & (k < fast)

            @pl.when(valid(c, m, me) & jnp.logical_not(is_early & (p == 0)))
            def _():
                @pl.when((p > 0) & jnp.logical_not(is_early & (p == 1)))
                def _():
                    y_inner(i, k).wait_recv()
                    u[i, q] = u[i, q] + below * yin[i, q].astype(jnp.float32)

                if fast:
                    @pl.when(is_early & (p == 1))
                    def _():
                        whole = jnp.zeros((hs, LANES), jnp.float32)
                        for d in range(R):
                            y_early(d, k).wait_recv()
                            whole += yd[d, q].astype(jnp.float32)
                        u[i, q] = u[i, q] + below * whole
                yb[i, q] = (u[i, q] * dd[slot, q]).astype(jnp.bfloat16)

                @pl.when(mid)
                def _():
                    y_middle(i, k).start()

                @pl.when(jnp.logical_not(mid))
                def _():
                    y_inner(i, k).start()

        @pl.when((at_u >= 0) & (at_u < total) & (at_u % S == 0))
        def _():
            i = at_u // S
            c, m = i // M, i % M

            @pl.when(i == 0)
            def _():
                consts[2].wait()

            @pl.when(valid(c, m, me))
            def _():
                for d in range(1, R):
                    row_out(i, d).wait_recv()
                u[i] = dot(th[...], fr[i].reshape(H, LANES))

        @pl.when((at_w >= 0) & (at_w < total) & (at_w % S == S - 1))
        def _():
            i = at_w // S
            c, m = i // M, i % M
            for d in range(1, R):
                @pl.when(valid(c, m, j * R + lax.rem(r + R - d, R)))
                def _():
                    row_back(i, c, m, d).wait_recv()
                    for e in range(1, J):
                        col_share(i, c, m, d, e).start()

        @pl.when((s < N * STRIDE) & (s % STRIDE == 0))
        def _():
            i = s // STRIDE
            c, m = i // M, i % M
            slot = slot_of(c, m)
            fresh = (c == 0) | (m == M - 1)

            @pl.when(fresh)
            def _():
                for rr in range(R):
                    table_wait(slot, rr).wait()

            def cols_of(d):
                return pl.ds(pl.multiple_of(lax.rem(j + J - d, J) * cols, 16), cols)
            first = dot(x[c], tf[slot, cols_of(0)])

            @pl.when(m == 0)
            def _():
                for d in range(1, J):
                    gather(c, d).wait_recv()
            acc = first
            for d in range(1, J):
                acc += dot(xg[c, d - 1], tf[slot, cols_of(d)])
            low = acc.astype(jnp.bfloat16)
            for rr in range(R):
                sw[i, rr] = low[:, rr * LANES:(rr + 1) * LANES]
            for d in range(1, R):
                @pl.when(valid(c, m, j * R + lax.rem(r + d, R)))
                def _():
                    row_out(i, d).start()
            fr[i, r] = sw[i, r]

            if fast:
                @pl.when((i == 0) & (p == 0))
                def _():
                    early.wait()
                    for d in range(R):
                        peer = lax.rem(r + d, R)
                        b = block(0, 0, j * R + peer)

                        @pl.when(b < B)
                        def _():
                            pivot = er[:ahead] + ec[jnp.minimum(b, B - 1)] + above
                            ys[peer] = (dot(tp[...], sw[0, peer]) * (1.0 / pivot)).astype(jnp.bfloat16)

                    for k in range(fast):
                        for d in range(R):
                            @pl.when(valid(0, 0, j * R + lax.rem(r + d, R)))
                            def _():
                                y_early(d, k).start()

                @pl.when((i == 0) & (p > 0))
                def _():
                    early.wait()

            for c_next in range(1, C):
                @pl.when(i == c_next - 1)
                def _():
                    blend(c_next)
                    for d in range(1, J):
                        gather(c_next, d).start()

            @pl.when(fresh & (i > 0))
            def _():
                build_pivots(c, m, slot)

        @pl.when((at_g >= 0) & (at_g < total) & (at_g % S == S - 1))
        def _():
            i = at_g // S
            c, m = i // M, i % M

            @pl.when(i == 0)
            def _():
                consts[4].wait()
            for d in range(R):
                for e in range(1, J):
                    @pl.when(valid(c, m, lax.rem(j + J - e, J) * R + lax.rem(r + R - d, R)))
                    def _():
                        col_share(i, c, m, d, e).wait_recv()

            if M > 1:
                @pl.when(m < M - 1)
                def _():
                    span = pl.ds(pl.multiple_of(m * D * LANES, LANES), D * LANES)
                    part = dot(rg[c, :, span], tb[span, :])

                    @pl.when(m == 0)
                    def _():
                        out[c] = part

                    @pl.when(m > 0)
                    def _():
                        out[c] = out[c] + part

            @pl.when(m == M - 1)
            def _():
                first = (M - 1) * D * LANES
                part = dot(rg[c, :, first:], tb[first:, :])
                out[c] = part if M == 1 else out[c] + part

            for d in range(1, R):
                @pl.when(valid(c, m, j * R + lax.rem(r + d, R)))
                def _():
                    row_out(i, d).wait_send()

                @pl.when(valid(c, m, j * R + lax.rem(r + R - d, R)))
                def _():
                    for e in range(1, J):
                        col_share(i, c, m, d, e).wait_send()

            @pl.when(valid(c, m, me))
            def _():
                for d in range(1, R):
                    row_back(i, c, m, d).wait_send()
                for e in range(1, J):
                    col_share(i, c, m, 0, e).wait_send()
                @pl.when((i > 0) | (p > 0))
                def _():
                    whole_wait(yb.at[i], y_s.at[i])

                @pl.when((i == 0) & (p == 0))
                def _():
                    if fast < S:
                        whole_wait(yb.at[0, pl.ds(ahead, H - ahead)], y_s.at[0])

                @pl.when(p > 0)
                def _():
                    whole_wait(xb.at[i], x_s.at[i])
        return carry

    lax.fori_loop(0, total + LAG_U + 1 + (HOP_UP + HOP_DOWN) * (half - 1) + HOP_MID + LAG_W + LAG_G, step, 0)
    for c in range(C):
        for d in range(1, J):
            gather(c, d).wait_send()

    @pl.when(p == 0)
    def _():
        for d in range(R):
            @pl.when(valid(0, 0, j * R + lax.rem(r + d, R)))
            def _():
                for k in range(fast):
                    y_early(d, k).wait_send()


def local(seams, levels, weights):
    _, C, rows, cols = seams.shape
    R, J, n = lax.axis_size("row"), lax.axis_size("col"), lax.axis_size("tm")
    H, W = rows * R, cols * J
    D = J * R
    B = W // LANES
    M = -(-B // D)
    N = C * M
    S = PARTS
    Q = M - 1 + C

    table_w, table_h = cosine_table(W), cosine_table(H)
    tab_f = jnp.asarray(np.ascontiguousarray(table_w.reshape(B, LANES, W).transpose(0, 2, 1)))
    tab_b = jnp.asarray(np.ascontiguousarray(table_w.reshape(W, J, cols).transpose(1, 0, 2)))
    tab_h = jnp.asarray(table_h)
    tab_t = jnp.asarray(np.ascontiguousarray(table_h.T).reshape(R, rows, H))
    tab_p = jnp.asarray(np.ascontiguousarray(table_h.reshape(H, R, rows).transpose(1, 0, 2)))
    eig_r = jnp.asarray(np.ascontiguousarray(
        np.broadcast_to((np.float32(screen) + laplace_eigen(H))[:, None], (H, LANES))))
    eig_c = jnp.asarray(laplace_eigen(W).reshape(B, 1, LANES))

    bf, f32 = jnp.bfloat16, jnp.float32
    vm, dma = pltpu.VMEM, pltpu.SemaphoreType.DMA
    hbm = pl.BlockSpec(memory_space=pltpu.HBM)
    result = pl.pallas_call(
        functools.partial(kernel, J, R, n, C, M, B, S),
        out_shape=pltpu.VMEM((C, rows, cols), f32),
        in_specs=[hbm] * 10,
        out_specs=pl.BlockSpec(memory_space=pltpu.VMEM),
        scratch_shapes=[
            pltpu.SMEM(levels.shape, jnp.int32),
            pltpu.SMEM(weights.shape, jnp.int32),
            vm((C, rows, cols), bf),
            vm((rows, cols), f32),
            vm((Q, W, R * LANES), bf),
            vm((W, cols), bf),
            vm((H, H), bf),
            vm((R, rows, H), bf),
            vm((max(FAST, 1) * (H // S), rows), bf),
            vm((R, max(FAST, 1) * (H // S), LANES), bf),
            vm((R, max(FAST, 1) * (H // S), LANES), bf),
            vm((H, LANES), f32),
            vm((B, 1, LANES), f32),
            vm((C, rows, cols), bf),
            vm((C, J - 1, rows, cols), bf),
            vm((N, R, rows, LANES), bf),
            vm((N, R, rows, LANES), bf),
            vm((Q, H, LANES), f32),
            vm((Q, H, LANES), f32),
            vm((N, H, LANES), f32),
            vm((N, H, LANES), bf),
            vm((N, H, LANES), bf),
            vm((N, H, LANES), bf),
            vm((N, H, LANES), bf),
            vm((N, R, rows, LANES), bf),
            vm((C, rows, W), bf),
            dma((C,)), dma((Q, R)), dma((8,)),
            dma((C, J - 1)), dma((C, J - 1)),
            dma((N, R - 1)), dma((N, R - 1)),
            dma((N,)), dma((N * S,)), dma((N * S,)), dma((N,)),
            dma((N, R - 1)), dma((N, R - 1)),
            dma((N, R, J - 1)), dma((N, R, J - 1)),
            dma((R, max(FAST, 1))), dma((R, max(FAST, 1))),
        ],
        compiler_params=pltpu.CompilerParams(
            collective_id=0, has_side_effects=True, vmem_limit_bytes=52 * 1024 * 1024),
    )(seams[0], levels, weights, tab_f, tab_b, tab_h, tab_t, tab_p, eig_r, eig_c)
    return result[None]


def solution(mesh):
    placed = (P(("win", "tm"), None, "row", "col"), P(("win", "tm"), "row", "col"), P("win"))
    return jax.shard_map(
        local,
        mesh=mesh,
        in_specs=placed,
        out_specs=P(("win", "tm"), None, "row", "col"),
        check_vma=False,
    )
```

```python
import functools
import math

import jax
import jax.numpy as jnp
import ml_dtypes
import numpy as np
from jax import lax
from jax.experimental import pallas as pl
from jax.experimental.pallas import tpu as pltpu
from jax.sharding import PartitionSpec as P

screen = 0.001
LANES = 128
PARTS = 3
HOP_UP = 4
HOP_MID = 4
HOP_DOWN = 4
FAST = 2
STRIDE = 2
LAG_U = 5
LAG_W = 6
LAG_G = 4
MESH = pl.DeviceIdType.MESH


def cosine_table(length):
    ids = np.arange(length, dtype=np.int64)
    phases = (2 * ids[None, :] + 1) * ids[:, None] % (4 * length)
    angles = phases.astype(np.float32) * np.float32(math.pi / (2.0 * length))
    scales = np.where(ids == 0, math.sqrt(1.0 / length), math.sqrt(2.0 / length)).astype(np.float32)
    table = np.cos(angles.astype(np.float64)).astype(np.float32) * scales[:, None]
    return table.astype(ml_dtypes.bfloat16)


def laplace_eigen(length):
    sines = np.sin(np.arange(length, dtype=np.float32) * np.float32(math.pi / (2.0 * length)))
    return np.float32(4.0) * sines * sines


def kernel(J, R, n, C, M, B, S, seams, levels_in, weights_in, tab_f, tab_b, tab_h, tab_t, tab_p, eig_r, eig_c, out,
           levels, weights, raw, grid, tf, tb, th, tt, tp, ys, yd, er, ec, x, xg, sw, fr, dd, ee, u, yb, yin, zin, xb, rs, rg,
           i_s, t_s, k_s, g_s, g_r, f_s, f_r, y_s, y_r, z_r, x_s, b_s, b_r, c_s, c_r, e_s, e_r):
    j, r, t = lax.axis_index("col"), lax.axis_index("row"), lax.axis_index("tm")
    N, D = C * M, J * R
    rows, cols = x.shape[1], x.shape[2]
    H = rows * R
    hs = H // S
    me = j * R + r
    left = t < n // 2
    half = n // 2
    p = jnp.where(left, t, n - 1 - t)
    inner = jnp.where(left, t + 1, t - 1)
    outer = jnp.where(left, t - 1, t + 1)
    mid = p == half - 1

    barrier = pltpu.get_barrier_semaphore()
    for d in range(1, J):
        pl.semaphore_signal(barrier, 1, device_id={"col": lax.rem(j + d, J)}, device_id_type=MESH)
    for d in range(1, R):
        pl.semaphore_signal(barrier, 1, device_id={"row": lax.rem(r + d, R)}, device_id_type=MESH)
    pl.semaphore_signal(barrier, 1, device_id={"tm": inner}, device_id_type=MESH)

    for d in range(1, R):
        pl.semaphore_signal(barrier, 1, device_id={"tm": inner, "row": lax.rem(r + d, R)}, device_id_type=MESH)

    @pl.when(p > 0)
    def _():
        pl.semaphore_signal(barrier, 1, device_id={"tm": outer}, device_id_type=MESH)
        for d in range(1, R):
            pl.semaphore_signal(barrier, 1, device_id={"tm": outer, "row": lax.rem(r + d, R)}, device_id_type=MESH)

    def block(c, m, d):
        return m * D + jnp.where(m == M - 1, lax.rem(d + c, D), d)

    def valid(c, m, d):
        return block(c, m, d) < B

    def slot_of(c, m):
        return jnp.where(m == M - 1, M - 1 + c, m)

    slots = [(0, m) for m in range(M)] + [(c, M - 1) for c in range(1, C)]

    def load(c):
        return pltpu.make_async_copy(seams.at[c], raw.at[c], i_s.at[c])

    def load_table(slot, rr):
        if isinstance(slot, int):
            c, m = slots[slot]
        b = jnp.minimum(block(c, m, j * R + rr), B - 1)
        return pltpu.make_async_copy(tab_f.at[b], tf.at[slot, :, rr * LANES:(rr + 1) * LANES], t_s.at[slot, rr])

    def table_wait(slot, rr):
        return pltpu.make_async_copy(tab_f.at[0], tf.at[slot, :, rr * LANES:(rr + 1) * LANES], t_s.at[slot, rr])

    consts = [pltpu.make_async_copy(s, d, k_s.at[k]) for k, (s, d) in enumerate(
        [(eig_r, er), (eig_c, ec), (tab_h, th), (tab_t, tt), (tab_b.at[j], tb),
         (levels_in, levels), (weights_in, weights)])]
    fast = min(FAST, S) if half > 1 else 0
    ahead = fast * hs
    if fast:
        early = pltpu.make_async_copy(tab_p.at[r, pl.ds(0, ahead)], tp, k_s.at[7])

    load(0).start()
    for k in range(5, 7):
        consts[k].start()
    for rr in range(R):
        load_table(0, rr).start()
    for k in range(2):
        consts[k].start()
    if fast:
        early.start()

    for k in range(5, 7):
        consts[k].wait()
    tile_rows, tile_cols = rows // levels.shape[1], cols // levels.shape[2]
    tile_of = lax.broadcasted_iota(jnp.int32, (1, cols), 1) // tile_cols
    for a in range(levels.shape[1]):
        line = jnp.zeros((1, cols), jnp.float32)
        for b in range(levels.shape[2]):
            line = jnp.where(tile_of == b, levels[0, a, b].astype(jnp.float32) * 0.25, line)
        grid[a * tile_rows:(a + 1) * tile_rows, :] = jnp.broadcast_to(line, (tile_rows, cols))

    stiff = [jnp.full((1, LANES), weights[k].astype(jnp.float32)) * (1.0 / 256.0) for k in range(n)]
    couple = [2.0 * stiff[k] * stiff[k + 1] / (stiff[k] + stiff[k + 1]) for k in range(n - 1)]
    zero = jnp.zeros((1, LANES), jnp.float32)
    ends, flipped = [zero] + couple, [zero] + couple[::-1]
    own = [jnp.where(left, a, b) for a, b in zip(ends, flipped)]
    other = [jnp.where(left, b, a) for a, b in zip(ends, flipped)]
    below, above = own[0], own[1]
    for k in range(1, half):
        below = jnp.where(p == k, own[k], below)
        above = jnp.where(p == k, own[k + 1], above)

    def blend(c):
        load(c).wait()
        x[c] = (raw[c].astype(jnp.float32) * grid[...]).astype(jnp.bfloat16)

    def build_pivots(c, m, slot):
        b = jnp.minimum(block(c, m, me), B - 1)
        a = er[...] + ec[b]

        def sweep(chain):
            rest, first = None, None
            for k in range(half):
                base = a if k == 0 else a + chain[k] * rest
                inverse = 1.0 / (base + chain[k + 1])
                first = inverse if k == 0 else jnp.where(p == k, inverse, first)
                rest = base * inverse
            return base, rest, first

        base, _, first = sweep(own)
        _, rest_other, _ = sweep(other)
        dd[slot] = first
        ee[slot] = jnp.where(p == half - 1, 1.0 / (base + own[half] * rest_other), first)

    def remote(src, dst, ss, rs_, where):
        return pltpu.make_async_remote_copy(
            src_ref=src, dst_ref=dst, send_sem=ss, recv_sem=rs_,
            device_id=where, device_id_type=MESH)

    def lanes_of(c, m, d):
        return pl.ds(pl.multiple_of(jnp.minimum(block(c, m, d), B - 1) * LANES, LANES), LANES)

    def q_of(k):
        return pl.ds(pl.multiple_of(k * hs, 16), hs)

    def gather(c, d):
        return remote(x.at[c], xg.at[c, d - 1], g_s.at[c, d - 1], g_r.at[c, d - 1],
                      {"col": lax.rem(j + d, J)})

    def row_out(i, d):
        peer = lax.rem(r + d, R)
        return remote(sw.at[i, peer], fr.at[i, r], f_s.at[i, d - 1], f_r.at[i, d - 1], {"row": peer})

    def y_inner(i, k):
        return remote(yb.at[i, q_of(k)], yin.at[i, q_of(k)], y_s.at[i], y_r.at[i * S + k], {"tm": inner})

    def y_early(d, k):
        peer = lax.rem(r + d, R)
        return remote(ys.at[peer, q_of(k)], yd.at[d, q_of(k)], e_s.at[d, k], e_r.at[d, k],
                      {"tm": inner, "row": peer})

    def y_middle(i, k):
        return remote(yb.at[i, q_of(k)], zin.at[i, q_of(k)], y_s.at[i], z_r.at[i * S + k], {"tm": inner})

    def x_outer(i, k):
        return remote(xb.at[i, q_of(k)], zin.at[i, q_of(k)], x_s.at[i], z_r.at[i * S + k], {"tm": outer})

    def row_back(i, c, m, d):
        peer = lax.rem(r + d, R)
        return remote(rs.at[i, peer], rg.at[c, :, lanes_of(c, m, me)], b_s.at[i, d - 1],
                      b_r.at[i, d - 1], {"row": peer})

    def col_share(i, c, m, d, e):
        part = rg.at[c, :, lanes_of(c, m, j * R + lax.rem(r + R - d, R))]
        return remote(part, part, c_s.at[i, d, e - 1], c_r.at[i, d, e - 1],
                      {"col": lax.rem(j + e, J)})

    def whole_wait(ref, sem):
        pltpu.make_async_copy(ref, ref, sem).wait()

    def dot(a, b):
        return jnp.dot(a, b, preferred_element_type=jnp.float32)

    blend(0)

    @pl.when(p > 0)
    def _():
        pl.semaphore_wait(barrier, J + R + 2 * (R - 1))

    @pl.when(p == 0)
    def _():
        pl.semaphore_wait(barrier, J + R - 1 + R - 1)

    for d in range(1, J):
        gather(0, d).start()
    for c in range(1, C):
        load(c).start()
    for slot in range(1, len(slots)):
        for rr in range(R):
            load_table(slot, rr).start()
        if slot == 1:
            consts[2].start()
    for k in range(3, 5):
        consts[k].start()
    for k in range(2):
        consts[k].wait()
    build_pivots(0, 0, 0 if M > 1 else M - 1)

    total = N * S

    def step(s, carry):
        at_u = s - LAG_U - HOP_UP * p
        at_y = at_u - 1
        at_x = s - LAG_U - 1 - HOP_UP * (half - 1) - HOP_MID - HOP_DOWN * (half - 1 - p)
        at_w = at_x - LAG_W
        at_g = at_w - LAG_G

        @pl.when((at_x >= 0) & (at_x < total))
        def _():
            i, k = at_x // S, at_x % S
            c, m = i // M, i % M
            slot = slot_of(c, m)
            q = q_of(k)

            @pl.when(valid(c, m, me))
            def _():
                x_outer(i, k).wait_recv()
                xb[i, q] = ((u[i, q] + above * zin[i, q].astype(jnp.float32)) * ee[slot, q]).astype(jnp.bfloat16)

                @pl.when(p > 0)
                def _():
                    x_outer(i, k).start()

                @pl.when(k == S - 1)
                def _():
                    @pl.when(i == 0)
                    def _():
                        consts[3].wait()
                    for d in range(1, R):
                        peer = lax.rem(r + d, R)
                        rs[i, peer] = dot(tt[peer], xb[i]).astype(jnp.bfloat16)
                        row_back(i, c, m, d).start()
                    rg[c, :, lanes_of(c, m, me)] = dot(tt[r], xb[i]).astype(jnp.bfloat16)
                    for e in range(1, J):
                        col_share(i, c, m, 0, e).start()

        @pl.when((at_y >= 0) & (at_y < total))
        def _():
            i, k = at_y // S, at_y % S
            c, m = i // M, i % M
            slot = slot_of(c, m)
            q = q_of(k)

            is_early = (i == 0) & (k < fast)

            @pl.when(valid(c, m, me) & jnp.logical_not(is_early & (p == 0)))
            def _():
                @pl.when((p > 0) & jnp.logical_not(is_early & (p == 1)))
                def _():
                    y_inner(i, k).wait_recv()
                    u[i, q] = u[i, q] + below * yin[i, q].astype(jnp.float32)

                if fast:
                    @pl.when(is_early & (p == 1))
                    def _():
                        whole = jnp.zeros((hs, LANES), jnp.float32)
                        for d in range(R):
                            y_early(d, k).wait_recv()
                            whole += yd[d, q].astype(jnp.float32)
                        u[i, q] = u[i, q] + below * whole
                yb[i, q] = (u[i, q] * dd[slot, q]).astype(jnp.bfloat16)

                @pl.when(mid)
                def _():
                    y_middle(i, k).start()

                @pl.when(jnp.logical_not(mid))
                def _():
                    y_inner(i, k).start()

        @pl.when((at_u >= 0) & (at_u < total) & (at_u % S == 0))
        def _():
            i = at_u // S
            c, m = i // M, i % M

            @pl.when(i == 0)
            def _():
                consts[2].wait()

            @pl.when(valid(c, m, me))
            def _():
                for d in range(1, R):
                    row_out(i, d).wait_recv()
                u[i] = dot(th[...], fr[i].reshape(H, LANES))

        @pl.when((at_w >= 0) & (at_w < total) & (at_w % S == S - 1))
        def _():
            i = at_w // S
            c, m = i // M, i % M
            for d in range(1, R):
                @pl.when(valid(c, m, j * R + lax.rem(r + R - d, R)))
                def _():
                    row_back(i, c, m, d).wait_recv()
                    for e in range(1, J):
                        col_share(i, c, m, d, e).start()

        @pl.when((s < N * STRIDE) & (s % STRIDE == 0))
        def _():
            i = s // STRIDE
            c, m = i // M, i % M
            slot = slot_of(c, m)
            fresh = (c == 0) | (m == M - 1)

            @pl.when(fresh)
            def _():
                for rr in range(R):
                    table_wait(slot, rr).wait()

            def cols_of(d):
                return pl.ds(pl.multiple_of(lax.rem(j + J - d, J) * cols, 16), cols)
            first = dot(x[c], tf[slot, cols_of(0)])

            @pl.when(m == 0)
            def _():
                for d in range(1, J):
                    gather(c, d).wait_recv()
            acc = first
            for d in range(1, J):
                acc += dot(xg[c, d - 1], tf[slot, cols_of(d)])
            low = acc.astype(jnp.bfloat16)
            for rr in range(R):
                sw[i, rr] = low[:, rr * LANES:(rr + 1) * LANES]
            for d in range(1, R):
                @pl.when(valid(c, m, j * R + lax.rem(r + d, R)))
                def _():
                    row_out(i, d).start()
            fr[i, r] = sw[i, r]

            if fast:
                @pl.when((i == 0) & (p == 0))
                def _():
                    early.wait()
                    for d in range(R):
                        peer = lax.rem(r + d, R)
                        b = block(0, 0, j * R + peer)

                        @pl.when(b < B)
                        def _():
                            pivot = er[:ahead] + ec[jnp.minimum(b, B - 1)] + above
                            ys[peer] = (dot(tp[...], sw[0, peer]) * (1.0 / pivot)).astype(jnp.bfloat16)

                    for k in range(fast):
                        for d in range(R):
                            @pl.when(valid(0, 0, j * R + lax.rem(r + d, R)))
                            def _():
                                y_early(d, k).start()

                @pl.when((i == 0) & (p > 0))
                def _():
                    early.wait()

            for c_next in range(1, C):
                @pl.when(i == c_next - 1)
                def _():
                    blend(c_next)
                    for d in range(1, J):
                        gather(c_next, d).start()

            @pl.when(fresh & (i > 0))
            def _():
                build_pivots(c, m, slot)

        @pl.when((at_g >= 0) & (at_g < total) & (at_g % S == S - 1))
        def _():
            i = at_g // S
            c, m = i // M, i % M

            @pl.when(i == 0)
            def _():
                consts[4].wait()
            for d in range(R):
                for e in range(1, J):
                    @pl.when(valid(c, m, lax.rem(j + J - e, J) * R + lax.rem(r + R - d, R)))
                    def _():
                        col_share(i, c, m, d, e).wait_recv()

            if M > 1:
                @pl.when(m < M - 1)
                def _():
                    span = pl.ds(pl.multiple_of(m * D * LANES, LANES), D * LANES)
                    part = dot(rg[c, :, span], tb[span, :])

                    @pl.when(m == 0)
                    def _():
                        out[c] = part

                    @pl.when(m > 0)
                    def _():
                        out[c] = out[c] + part

            @pl.when(m == M - 1)
            def _():
                first = (M - 1) * D * LANES
                part = dot(rg[c, :, first:], tb[first:, :])
                out[c] = part if M == 1 else out[c] + part

            for d in range(1, R):
                @pl.when(valid(c, m, j * R + lax.rem(r + d, R)))
                def _():
                    row_out(i, d).wait_send()

                @pl.when(valid(c, m, j * R + lax.rem(r + R - d, R)))
                def _():
                    for e in range(1, J):
                        col_share(i, c, m, d, e).wait_send()

            @pl.when(valid(c, m, me))
            def _():
                for d in range(1, R):
                    row_back(i, c, m, d).wait_send()
                for e in range(1, J):
                    col_share(i, c, m, 0, e).wait_send()
                @pl.when((i > 0) | (p > 0))
                def _():
                    whole_wait(yb.at[i], y_s.at[i])

                @pl.when((i == 0) & (p == 0))
                def _():
                    if fast < S:
                        whole_wait(yb.at[0, pl.ds(ahead, H - ahead)], y_s.at[0])

                @pl.when(p > 0)
                def _():
                    whole_wait(xb.at[i], x_s.at[i])
        return carry

    lax.fori_loop(0, total + LAG_U + 1 + (HOP_UP + HOP_DOWN) * (half - 1) + HOP_MID + LAG_W + LAG_G, step, 0)
    for c in range(C):
        for d in range(1, J):
            gather(c, d).wait_send()

    @pl.when(p == 0)
    def _():
        for d in range(R):
            @pl.when(valid(0, 0, j * R + lax.rem(r + d, R)))
            def _():
                for k in range(fast):
                    y_early(d, k).wait_send()


def local(seams, levels, weights):
    _, C, rows, cols = seams.shape
    R, J, n = lax.axis_size("row"), lax.axis_size("col"), lax.axis_size("tm")
    H, W = rows * R, cols * J
    D = J * R
    B = W // LANES
    M = -(-B // D)
    N = C * M
    S = PARTS
    Q = M - 1 + C

    table_w, table_h = cosine_table(W), cosine_table(H)
    tab_f = jnp.asarray(np.ascontiguousarray(table_w.reshape(B, LANES, W).transpose(0, 2, 1)))
    tab_b = jnp.asarray(np.ascontiguousarray(table_w.reshape(W, J, cols).transpose(1, 0, 2)))
    tab_h = jnp.asarray(table_h)
    tab_t = jnp.asarray(np.ascontiguousarray(table_h.T).reshape(R, rows, H))
    tab_p = jnp.asarray(np.ascontiguousarray(table_h.reshape(H, R, rows).transpose(1, 0, 2)))
    eig_r = jnp.asarray(np.ascontiguousarray(
        np.broadcast_to((np.float32(screen) + laplace_eigen(H))[:, None], (H, LANES))))
    eig_c = jnp.asarray(laplace_eigen(W).reshape(B, 1, LANES))

    bf, f32 = jnp.bfloat16, jnp.float32
    vm, dma = pltpu.VMEM, pltpu.SemaphoreType.DMA
    hbm = pl.BlockSpec(memory_space=pltpu.HBM)
    result = pl.pallas_call(
        functools.partial(kernel, J, R, n, C, M, B, S),
        out_shape=pltpu.VMEM((C, rows, cols), f32),
        in_specs=[hbm] * 10,
        out_specs=pl.BlockSpec(memory_space=pltpu.VMEM),
        scratch_shapes=[
            pltpu.SMEM(levels.shape, jnp.int32),
            pltpu.SMEM(weights.shape, jnp.int32),
            vm((C, rows, cols), bf),
            vm((rows, cols), f32),
            vm((Q, W, R * LANES), bf),
            vm((W, cols), bf),
            vm((H, H), bf),
            vm((R, rows, H), bf),
            vm((max(FAST, 1) * (H // S), rows), bf),
            vm((R, max(FAST, 1) * (H // S), LANES), bf),
            vm((R, max(FAST, 1) * (H // S), LANES), bf),
            vm((H, LANES), f32),
            vm((B, 1, LANES), f32),
            vm((C, rows, cols), bf),
            vm((C, J - 1, rows, cols), bf),
            vm((N, R, rows, LANES), bf),
            vm((N, R, rows, LANES), bf),
            vm((Q, H, LANES), f32),
            vm((Q, H, LANES), f32),
            vm((N, H, LANES), f32),
            vm((N, H, LANES), bf),
            vm((N, H, LANES), bf),
            vm((N, H, LANES), bf),
            vm((N, H, LANES), bf),
            vm((N, R, rows, LANES), bf),
            vm((C, rows, W), bf),
            dma((C,)), dma((Q, R)), dma((8,)),
            dma((C, J - 1)), dma((C, J - 1)),
            dma((N, R - 1)), dma((N, R - 1)),
            dma((N,)), dma((N * S,)), dma((N * S,)), dma((N,)),
            dma((N, R - 1)), dma((N, R - 1)),
            dma((N, R, J - 1)), dma((N, R, J - 1)),
            dma((R, max(FAST, 1))), dma((R, max(FAST, 1))),
        ],
        compiler_params=pltpu.CompilerParams(
            collective_id=0, has_side_effects=True, vmem_limit_bytes=52 * 1024 * 1024),
    )(seams[0], levels, weights, tab_f, tab_b, tab_h, tab_t, tab_p, eig_r, eig_c)
    return result[None]


def solution(mesh):
    placed = (P(("win", "tm"), None, "row", "col"), P(("win", "tm"), "row", "col"), P("win"))
    return jax.shard_map(
        local,
        mesh=mesh,
        in_specs=placed,
        out_specs=P(("win", "tm"), None, "row", "col"),
        check_vma=False,
    )
```

```python
import functools
import math

import jax
import jax.numpy as jnp
import ml_dtypes
import numpy as np
from jax import lax
from jax.experimental import pallas as pl
from jax.experimental.pallas import tpu as pltpu
from jax.sharding import PartitionSpec as P

screen = 0.001
LANES = 128
PARTS = 3
HOP_UP = 4
HOP_MID = 4
HOP_DOWN = 4
FAST = 2
STRIDE = 2
LAG_U = 5
LAG_W = 6
LAG_G = 4
MESH = pl.DeviceIdType.MESH


def cosine_table(length):
    ids = np.arange(length, dtype=np.int64)
    phases = (2 * ids[None, :] + 1) * ids[:, None] % (4 * length)
    angles = phases.astype(np.float32) * np.float32(math.pi / (2.0 * length))
    scales = np.where(ids == 0, math.sqrt(1.0 / length), math.sqrt(2.0 / length)).astype(np.float32)
    table = np.cos(angles.astype(np.float64)).astype(np.float32) * scales[:, None]
    return table.astype(ml_dtypes.bfloat16)


def laplace_eigen(length):
    sines = np.sin(np.arange(length, dtype=np.float32) * np.float32(math.pi / (2.0 * length)))
    return np.float32(4.0) * sines * sines


def kernel(J, R, n, C, M, B, S, seams, levels_in, weights_in, tab_f, tab_b, tab_h, tab_t, tab_p, eig_r, eig_c, out, back_out, table_out,
           levels, weights, raw, grid, tf, tb, th, tt, tp, ys, yd, er, ec, x, xg, sw, fr, dd, ee, u, yb, yin, zin, xb, rs, rg,
           i_s, t_s, k_s, g_s, g_r, f_s, f_r, y_s, y_r, z_r, x_s, b_s, b_r, c_s, c_r, e_s, e_r):
    j, r, t = lax.axis_index("col"), lax.axis_index("row"), lax.axis_index("tm")
    N, D = C * M, J * R
    rows, cols = x.shape[1], x.shape[2]
    H = rows * R
    hs = H // S
    me = j * R + r
    left = t < n // 2
    half = n // 2
    p = jnp.where(left, t, n - 1 - t)
    inner = jnp.where(left, t + 1, t - 1)
    outer = jnp.where(left, t - 1, t + 1)
    mid = p == half - 1

    barrier = pltpu.get_barrier_semaphore()
    for d in range(1, J):
        pl.semaphore_signal(barrier, 1, device_id={"col": lax.rem(j + d, J)}, device_id_type=MESH)
    for d in range(1, R):
        pl.semaphore_signal(barrier, 1, device_id={"row": lax.rem(r + d, R)}, device_id_type=MESH)
    pl.semaphore_signal(barrier, 1, device_id={"tm": inner}, device_id_type=MESH)

    for d in range(1, R):
        pl.semaphore_signal(barrier, 1, device_id={"tm": inner, "row": lax.rem(r + d, R)}, device_id_type=MESH)

    @pl.when(p > 0)
    def _():
        pl.semaphore_signal(barrier, 1, device_id={"tm": outer}, device_id_type=MESH)
        for d in range(1, R):
            pl.semaphore_signal(barrier, 1, device_id={"tm": outer, "row": lax.rem(r + d, R)}, device_id_type=MESH)

    def block(c, m, d):
        return m * D + jnp.where(m == M - 1, lax.rem(d + c, D), d)

    def valid(c, m, d):
        return block(c, m, d) < B

    def slot_of(c, m):
        return jnp.where(m == M - 1, M - 1 + c, m)

    slots = [(0, m) for m in range(M)] + [(c, M - 1) for c in range(1, C)]

    def load(c):
        return pltpu.make_async_copy(seams.at[c], raw.at[c], i_s.at[c])

    def load_table(slot, rr):
        if isinstance(slot, int):
            c, m = slots[slot]
        b = jnp.minimum(block(c, m, j * R + rr), B - 1)
        return pltpu.make_async_copy(tab_f.at[b], tf.at[slot, :, rr * LANES:(rr + 1) * LANES], t_s.at[slot, rr])

    def table_wait(slot, rr):
        return pltpu.make_async_copy(tab_f.at[0], tf.at[slot, :, rr * LANES:(rr + 1) * LANES], t_s.at[slot, rr])

    consts = [pltpu.make_async_copy(s, d, k_s.at[k]) for k, (s, d) in enumerate(
        [(eig_r, er), (eig_c, ec), (tab_h, th), (tab_t, tt), (tab_b.at[j], tb),
         (levels_in, levels), (weights_in, weights)])]
    first_last = (M - 1) * D * LANES
    ending = pltpu.make_async_copy(tab_b.at[j, pl.ds(first_last, B * LANES - first_last)], table_out, k_s.at[8])
    fast = min(FAST, S) if half > 1 else 0
    ahead = fast * hs
    if fast:
        early = pltpu.make_async_copy(tab_p.at[r, pl.ds(0, ahead)], tp, k_s.at[7])

    load(0).start()
    for k in range(5, 7):
        consts[k].start()
    for rr in range(R):
        load_table(0, rr).start()
    for k in range(2):
        consts[k].start()
    if fast:
        early.start()

    for k in range(5, 7):
        consts[k].wait()
    tile_rows, tile_cols = rows // levels.shape[1], cols // levels.shape[2]
    tile_of = lax.broadcasted_iota(jnp.int32, (1, cols), 1) // tile_cols
    for a in range(levels.shape[1]):
        line = jnp.zeros((1, cols), jnp.float32)
        for b in range(levels.shape[2]):
            line = jnp.where(tile_of == b, levels[0, a, b].astype(jnp.float32) * 0.25, line)
        grid[a * tile_rows:(a + 1) * tile_rows, :] = jnp.broadcast_to(line, (tile_rows, cols))

    stiff = [jnp.full((1, LANES), weights[k].astype(jnp.float32)) * (1.0 / 256.0) for k in range(n)]
    couple = [2.0 * stiff[k] * stiff[k + 1] / (stiff[k] + stiff[k + 1]) for k in range(n - 1)]
    zero = jnp.zeros((1, LANES), jnp.float32)
    ends, flipped = [zero] + couple, [zero] + couple[::-1]
    own = [jnp.where(left, a, b) for a, b in zip(ends, flipped)]
    other = [jnp.where(left, b, a) for a, b in zip(ends, flipped)]
    below, above = own[0], own[1]
    for k in range(1, half):
        below = jnp.where(p == k, own[k], below)
        above = jnp.where(p == k, own[k + 1], above)

    def blend(c):
        load(c).wait()
        x[c] = (raw[c].astype(jnp.float32) * grid[...]).astype(jnp.bfloat16)

    def build_pivots(c, m, slot):
        b = jnp.minimum(block(c, m, me), B - 1)
        a = er[...] + ec[b]

        def sweep(chain):
            rest, first = None, None
            for k in range(half):
                base = a if k == 0 else a + chain[k] * rest
                inverse = 1.0 / (base + chain[k + 1])
                first = inverse if k == 0 else jnp.where(p == k, inverse, first)
                rest = base * inverse
            return base, rest, first

        base, _, first = sweep(own)
        _, rest_other, _ = sweep(other)
        dd[slot] = first
        ee[slot] = jnp.where(p == half - 1, 1.0 / (base + own[half] * rest_other), first)

    def remote(src, dst, ss, rs_, where):
        return pltpu.make_async_remote_copy(
            src_ref=src, dst_ref=dst, send_sem=ss, recv_sem=rs_,
            device_id=where, device_id_type=MESH)

    def lanes_of(c, m, d):
        return pl.ds(pl.multiple_of(jnp.minimum(block(c, m, d), B - 1) * LANES, LANES), LANES)

    def q_of(k):
        return pl.ds(pl.multiple_of(k * hs, 16), hs)

    def gather(c, d):
        return remote(x.at[c], xg.at[c, d - 1], g_s.at[c, d - 1], g_r.at[c, d - 1],
                      {"col": lax.rem(j + d, J)})

    def row_out(i, d):
        peer = lax.rem(r + d, R)
        return remote(sw.at[i, peer], fr.at[i, r], f_s.at[i, d - 1], f_r.at[i, d - 1], {"row": peer})

    def y_inner(i, k):
        return remote(yb.at[i, q_of(k)], yin.at[i, q_of(k)], y_s.at[i], y_r.at[i * S + k], {"tm": inner})

    def y_early(d, k):
        peer = lax.rem(r + d, R)
        return remote(ys.at[peer, q_of(k)], yd.at[d, q_of(k)], e_s.at[d, k], e_r.at[d, k],
                      {"tm": inner, "row": peer})

    def y_middle(i, k):
        return remote(yb.at[i, q_of(k)], zin.at[i, q_of(k)], y_s.at[i], z_r.at[i * S + k], {"tm": inner})

    def x_outer(i, k):
        return remote(xb.at[i, q_of(k)], zin.at[i, q_of(k)], x_s.at[i], z_r.at[i * S + k], {"tm": outer})

    def row_back(i, c, m, d):
        peer = lax.rem(r + d, R)
        return remote(rs.at[i, peer], rg.at[c, :, lanes_of(c, m, me)], b_s.at[i, d - 1],
                      b_r.at[i, d - 1], {"row": peer})

    def col_share(i, c, m, d, e):
        part = rg.at[c, :, lanes_of(c, m, j * R + lax.rem(r + R - d, R))]
        return remote(part, part, c_s.at[i, d, e - 1], c_r.at[i, d, e - 1],
                      {"col": lax.rem(j + e, J)})

    def whole_wait(ref, sem):
        pltpu.make_async_copy(ref, ref, sem).wait()

    def dot(a, b):
        return jnp.dot(a, b, preferred_element_type=jnp.float32)

    blend(0)

    @pl.when(p > 0)
    def _():
        pl.semaphore_wait(barrier, J + R + 2 * (R - 1))

    @pl.when(p == 0)
    def _():
        pl.semaphore_wait(barrier, J + R - 1 + R - 1)

    for d in range(1, J):
        gather(0, d).start()
    for c in range(1, C):
        load(c).start()
    for slot in range(1, len(slots)):
        for rr in range(R):
            load_table(slot, rr).start()
        if slot == 1:
            consts[2].start()
    for k in range(3, 5):
        consts[k].start()
    ending.start()
    for k in range(2):
        consts[k].wait()
    build_pivots(0, 0, 0 if M > 1 else M - 1)

    total = N * S

    def step(s, carry):
        at_u = s - LAG_U - HOP_UP * p
        at_y = at_u - 1
        at_x = s - LAG_U - 1 - HOP_UP * (half - 1) - HOP_MID - HOP_DOWN * (half - 1 - p)
        at_w = at_x - LAG_W
        at_g = at_w - LAG_G

        @pl.when((at_x >= 0) & (at_x < total))
        def _():
            i, k = at_x // S, at_x % S
            c, m = i // M, i % M
            slot = slot_of(c, m)
            q = q_of(k)

            @pl.when(valid(c, m, me))
            def _():
                x_outer(i, k).wait_recv()
                xb[i, q] = ((u[i, q] + above * zin[i, q].astype(jnp.float32)) * ee[slot, q]).astype(jnp.bfloat16)

                @pl.when(p > 0)
                def _():
                    x_outer(i, k).start()

                @pl.when(k == S - 1)
                def _():
                    @pl.when(i == 0)
                    def _():
                        consts[3].wait()
                    for d in range(1, R):
                        peer = lax.rem(r + d, R)
                        rs[i, peer] = dot(tt[peer], xb[i]).astype(jnp.bfloat16)
                        row_back(i, c, m, d).start()
                    rg[c, :, lanes_of(c, m, me)] = dot(tt[r], xb[i]).astype(jnp.bfloat16)
                    for e in range(1, J):
                        col_share(i, c, m, 0, e).start()

        @pl.when((at_y >= 0) & (at_y < total))
        def _():
            i, k = at_y // S, at_y % S
            c, m = i // M, i % M
            slot = slot_of(c, m)
            q = q_of(k)

            is_early = (i == 0) & (k < fast)

            @pl.when(valid(c, m, me) & jnp.logical_not(is_early & (p == 0)))
            def _():
                @pl.when((p > 0) & jnp.logical_not(is_early & (p == 1)))
                def _():
                    y_inner(i, k).wait_recv()
                    u[i, q] = u[i, q] + below * yin[i, q].astype(jnp.float32)

                if fast:
                    @pl.when(is_early & (p == 1))
                    def _():
                        whole = jnp.zeros((hs, LANES), jnp.float32)
                        for d in range(R):
                            y_early(d, k).wait_recv()
                            whole += yd[d, q].astype(jnp.float32)
                        u[i, q] = u[i, q] + below * whole
                yb[i, q] = (u[i, q] * dd[slot, q]).astype(jnp.bfloat16)

                @pl.when(mid)
                def _():
                    y_middle(i, k).start()

                @pl.when(jnp.logical_not(mid))
                def _():
                    y_inner(i, k).start()

        @pl.when((at_u >= 0) & (at_u < total) & (at_u % S == 0))
        def _():
            i = at_u // S
            c, m = i // M, i % M

            @pl.when(i == 0)
            def _():
                consts[2].wait()

            @pl.when(valid(c, m, me))
            def _():
                for d in range(1, R):
                    row_out(i, d).wait_recv()
                u[i] = dot(th[...], fr[i].reshape(H, LANES))

        @pl.when((at_w >= 0) & (at_w < total) & (at_w % S == S - 1))
        def _():
            i = at_w // S
            c, m = i // M, i % M
            for d in range(1, R):
                @pl.when(valid(c, m, j * R + lax.rem(r + R - d, R)))
                def _():
                    row_back(i, c, m, d).wait_recv()
                    for e in range(1, J):
                        col_share(i, c, m, d, e).start()

        @pl.when((s < N * STRIDE) & (s % STRIDE == 0))
        def _():
            i = s // STRIDE
            c, m = i // M, i % M
            slot = slot_of(c, m)
            fresh = (c == 0) | (m == M - 1)

            @pl.when(fresh)
            def _():
                for rr in range(R):
                    table_wait(slot, rr).wait()

            def cols_of(d):
                return pl.ds(pl.multiple_of(lax.rem(j + J - d, J) * cols, 16), cols)
            first = dot(x[c], tf[slot, cols_of(0)])

            @pl.when(m == 0)
            def _():
                for d in range(1, J):
                    gather(c, d).wait_recv()
            acc = first
            for d in range(1, J):
                acc += dot(xg[c, d - 1], tf[slot, cols_of(d)])
            low = acc.astype(jnp.bfloat16)
            for rr in range(R):
                sw[i, rr] = low[:, rr * LANES:(rr + 1) * LANES]
            for d in range(1, R):
                @pl.when(valid(c, m, j * R + lax.rem(r + d, R)))
                def _():
                    row_out(i, d).start()
            fr[i, r] = sw[i, r]

            if fast:
                @pl.when((i == 0) & (p == 0))
                def _():
                    early.wait()
                    for d in range(R):
                        peer = lax.rem(r + d, R)
                        b = block(0, 0, j * R + peer)

                        @pl.when(b < B)
                        def _():
                            pivot = er[:ahead] + ec[jnp.minimum(b, B - 1)] + above
                            ys[peer] = (dot(tp[...], sw[0, peer]) * (1.0 / pivot)).astype(jnp.bfloat16)

                    for k in range(fast):
                        for d in range(R):
                            @pl.when(valid(0, 0, j * R + lax.rem(r + d, R)))
                            def _():
                                y_early(d, k).start()

                @pl.when((i == 0) & (p > 0))
                def _():
                    early.wait()

            for c_next in range(1, C):
                @pl.when(i == c_next - 1)
                def _():
                    blend(c_next)
                    for d in range(1, J):
                        gather(c_next, d).start()

            @pl.when(fresh & (i > 0))
            def _():
                build_pivots(c, m, slot)

        @pl.when((at_g >= 0) & (at_g < total) & (at_g % S == S - 1))
        def _():
            i = at_g // S
            c, m = i // M, i % M

            @pl.when(i == 0)
            def _():
                consts[4].wait()
                ending.wait()
            for d in range(R):
                for e in range(1, J):
                    @pl.when(valid(c, m, lax.rem(j + J - e, J) * R + lax.rem(r + R - d, R)))
                    def _():
                        col_share(i, c, m, d, e).wait_recv()

            if M > 1:
                @pl.when(m < M - 1)
                def _():
                    span = pl.ds(pl.multiple_of(m * D * LANES, LANES), D * LANES)
                    part = dot(rg[c, :, span], tb[span, :])

                    @pl.when(m == 0)
                    def _():
                        out[c] = part

                    @pl.when(m > 0)
                    def _():
                        out[c] = out[c] + part

            @pl.when((m == M - 1) & (i < N - 1))
            def _():
                part = dot(rg[c, :, first_last:], tb[first_last:, :])
                out[c] = part if M == 1 else out[c] + part

            @pl.when(i == N - 1)
            def _():
                back_out[...] = rg[C - 1, :, first_last:]

            for d in range(1, R):
                @pl.when(valid(c, m, j * R + lax.rem(r + d, R)))
                def _():
                    row_out(i, d).wait_send()

                @pl.when(valid(c, m, j * R + lax.rem(r + R - d, R)))
                def _():
                    for e in range(1, J):
                        col_share(i, c, m, d, e).wait_send()

            @pl.when(valid(c, m, me))
            def _():
                for d in range(1, R):
                    row_back(i, c, m, d).wait_send()
                for e in range(1, J):
                    col_share(i, c, m, 0, e).wait_send()
                @pl.when((i > 0) | (p > 0))
                def _():
                    whole_wait(yb.at[i], y_s.at[i])

                @pl.when((i == 0) & (p == 0))
                def _():
                    if fast < S:
                        whole_wait(yb.at[0, pl.ds(ahead, H - ahead)], y_s.at[0])

                @pl.when(p > 0)
                def _():
                    whole_wait(xb.at[i], x_s.at[i])
        return carry

    lax.fori_loop(0, total + LAG_U + 1 + (HOP_UP + HOP_DOWN) * (half - 1) + HOP_MID + LAG_W + LAG_G, step, 0)
    for c in range(C):
        for d in range(1, J):
            gather(c, d).wait_send()

    @pl.when(p == 0)
    def _():
        for d in range(R):
            @pl.when(valid(0, 0, j * R + lax.rem(r + d, R)))
            def _():
                for k in range(fast):
                    y_early(d, k).wait_send()


def finish(M, pieces, held, back, table, out, total, sems):
    C, rows, _ = held.shape
    copies = [pltpu.make_async_copy(held.at[c], out.at[c], sems.at[c]) for c in range(C - 1)]
    for copy in copies:
        copy.start()
    each = rows // pieces
    for a in range(pieces):
        at = pl.ds(a * each, each)
        part = jnp.dot(back[at, :], table[...], preferred_element_type=jnp.float32)
        total[at, :] = part if M == 1 else held[C - 1, at, :] + part
        copy = pltpu.make_async_copy(total.at[at], out.at[C - 1, at], sems.at[C - 1 + a])
        copy.start()
        copies.append(copy)
    for copy in copies:
        copy.wait()


def local(seams, levels, weights):
    _, C, rows, cols = seams.shape
    R, J, n = lax.axis_size("row"), lax.axis_size("col"), lax.axis_size("tm")
    H, W = rows * R, cols * J
    D = J * R
    B = W // LANES
    M = -(-B // D)
    N = C * M
    S = PARTS
    Q = M - 1 + C

    table_w, table_h = cosine_table(W), cosine_table(H)
    tab_f = jnp.asarray(np.ascontiguousarray(table_w.reshape(B, LANES, W).transpose(0, 2, 1)))
    tab_b = jnp.asarray(np.ascontiguousarray(table_w.reshape(W, J, cols).transpose(1, 0, 2)))
    tab_h = jnp.asarray(table_h)
    tab_t = jnp.asarray(np.ascontiguousarray(table_h.T).reshape(R, rows, H))
    tab_p = jnp.asarray(np.ascontiguousarray(table_h.reshape(H, R, rows).transpose(1, 0, 2)))
    eig_r = jnp.asarray(np.ascontiguousarray(
        np.broadcast_to((np.float32(screen) + laplace_eigen(H))[:, None], (H, LANES))))
    eig_c = jnp.asarray(laplace_eigen(W).reshape(B, 1, LANES))

    bf, f32 = jnp.bfloat16, jnp.float32
    tail = W - (M - 1) * D * LANES
    pieces = 2 if rows % 32 == 0 else 1
    vm, dma = pltpu.VMEM, pltpu.SemaphoreType.DMA
    hbm = pl.BlockSpec(memory_space=pltpu.HBM)
    results = pl.pallas_call(
        functools.partial(kernel, J, R, n, C, M, B, S),
        out_shape=(pltpu.VMEM((C, rows, cols), f32), pltpu.VMEM((rows, tail), bf), pltpu.VMEM((tail, cols), bf)),
        in_specs=[hbm] * 10,
        out_specs=[pl.BlockSpec(memory_space=pltpu.VMEM)] * 3,
        scratch_shapes=[
            pltpu.SMEM(levels.shape, jnp.int32),
            pltpu.SMEM(weights.shape, jnp.int32),
            vm((C, rows, cols), bf),
            vm((rows, cols), f32),
            vm((Q, W, R * LANES), bf),
            vm((W, cols), bf),
            vm((H, H), bf),
            vm((R, rows, H), bf),
            vm((max(FAST, 1) * (H // S), rows), bf),
            vm((R, max(FAST, 1) * (H // S), LANES), bf),
            vm((R, max(FAST, 1) * (H // S), LANES), bf),
            vm((H, LANES), f32),
            vm((B, 1, LANES), f32),
            vm((C, rows, cols), bf),
            vm((C, J - 1, rows, cols), bf),
            vm((N, R, rows, LANES), bf),
            vm((N, R, rows, LANES), bf),
            vm((Q, H, LANES), f32),
            vm((Q, H, LANES), f32),
            vm((N, H, LANES), f32),
            vm((N, H, LANES), bf),
            vm((N, H, LANES), bf),
            vm((N, H, LANES), bf),
            vm((N, H, LANES), bf),
            vm((N, R, rows, LANES), bf),
            vm((C, rows, W), bf),
            dma((C,)), dma((Q, R)), dma((9,)),
            dma((C, J - 1)), dma((C, J - 1)),
            dma((N, R - 1)), dma((N, R - 1)),
            dma((N,)), dma((N * S,)), dma((N * S,)), dma((N,)),
            dma((N, R - 1)), dma((N, R - 1)),
            dma((N, R, J - 1)), dma((N, R, J - 1)),
            dma((R, max(FAST, 1))), dma((R, max(FAST, 1))),
        ],
        compiler_params=pltpu.CompilerParams(
            collective_id=0, has_side_effects=True, vmem_limit_bytes=52 * 1024 * 1024),
    )(seams[0], levels, weights, tab_f, tab_b, tab_h, tab_t, tab_p, eig_r, eig_c)
    held = [pltpu.with_memory_space_constraint(v, pltpu.VMEM) for v in results]
    return pl.pallas_call(
        functools.partial(finish, M, pieces),
        out_shape=jax.ShapeDtypeStruct((C, rows, cols), f32),
        in_specs=[pl.BlockSpec(memory_space=pltpu.VMEM)] * 3,
        out_specs=hbm,
        scratch_shapes=[vm((rows, cols), f32), dma((C - 1 + pieces,))],
        compiler_params=pltpu.CompilerParams(vmem_limit_bytes=6 * 1024 * 1024),
    )(*held)[None]


def solution(mesh):
    placed = (P(("win", "tm"), None, "row", "col"), P(("win", "tm"), "row", "col"), P("win"))
    return jax.shard_map(
        local,
        mesh=mesh,
        in_specs=placed,
        out_specs=P(("win", "tm"), None, "row", "col"),
        check_vma=False,
    )
```

```python
import functools
import math

import jax
import jax.numpy as jnp
import ml_dtypes
import numpy as np
from jax import lax
from jax.experimental import pallas as pl
from jax.experimental.pallas import tpu as pltpu
from jax.sharding import PartitionSpec as P

screen = 0.001
LANES = 128
PARTS = 3
HOP_UP = 4
HOP_MID = 4
HOP_DOWN = 4
FAST = 2
STRIDE = 2
LAG_U = 5
LAG_W = 6
LAG_G = 4
MESH = pl.DeviceIdType.MESH


def cosine_table(length):
    ids = np.arange(length, dtype=np.int64)
    phases = (2 * ids[None, :] + 1) * ids[:, None] % (4 * length)
    angles = phases.astype(np.float32) * np.float32(math.pi / (2.0 * length))
    scales = np.where(ids == 0, math.sqrt(1.0 / length), math.sqrt(2.0 / length)).astype(np.float32)
    table = np.cos(angles.astype(np.float64)).astype(np.float32) * scales[:, None]
    return table.astype(ml_dtypes.bfloat16)


def laplace_eigen(length):
    sines = np.sin(np.arange(length, dtype=np.float32) * np.float32(math.pi / (2.0 * length)))
    return np.float32(4.0) * sines * sines


def kernel(J, R, n, C, M, B, S, seams, levels_in, weights_in, tab_f, tab_b, tab_h, tab_t, tab_p, eig_r, eig_c, out, back_out, table_out,
           levels, weights, raw, grid, tf, tb, th, tt, tp, ys, yd, er, ec, x, xg, sw, fr, dd, ee, u, yb, yin, zin, xb, rs, rg,
           i_s, t_s, k_s, g_s, g_r, f_s, f_r, y_s, y_r, z_r, x_s, b_s, b_r, c_s, c_r, e_s, e_r):
    j, r, t = lax.axis_index("col"), lax.axis_index("row"), lax.axis_index("tm")
    N, D = C * M, J * R
    rows, cols = x.shape[1], x.shape[2]
    H = rows * R
    hs = H // S
    me = j * R + r
    left = t < n // 2
    half = n // 2
    p = jnp.where(left, t, n - 1 - t)
    inner = jnp.where(left, t + 1, t - 1)
    outer = jnp.where(left, t - 1, t + 1)
    mid = p == half - 1

    barrier = pltpu.get_barrier_semaphore()
    for d in range(1, J):
        pl.semaphore_signal(barrier, 1, device_id={"col": lax.rem(j + d, J)}, device_id_type=MESH)
    for d in range(1, R):
        pl.semaphore_signal(barrier, 1, device_id={"row": lax.rem(r + d, R)}, device_id_type=MESH)
    pl.semaphore_signal(barrier, 1, device_id={"tm": inner}, device_id_type=MESH)

    for d in range(1, R):
        pl.semaphore_signal(barrier, 1, device_id={"tm": inner, "row": lax.rem(r + d, R)}, device_id_type=MESH)

    @pl.when(p > 0)
    def _():
        pl.semaphore_signal(barrier, 1, device_id={"tm": outer}, device_id_type=MESH)
        for d in range(1, R):
            pl.semaphore_signal(barrier, 1, device_id={"tm": outer, "row": lax.rem(r + d, R)}, device_id_type=MESH)

    def block(c, m, d):
        return m * D + jnp.where(m == M - 1, lax.rem(d + c, D), d)

    def valid(c, m, d):
        return block(c, m, d) < B

    def slot_of(c, m):
        return jnp.where(m == M - 1, M - 1 + c, m)

    slots = [(0, m) for m in range(M)] + [(c, M - 1) for c in range(1, C)]

    def load(c):
        return pltpu.make_async_copy(seams.at[c], raw.at[c], i_s.at[c])

    def load_table(slot, rr):
        if isinstance(slot, int):
            c, m = slots[slot]
        b = jnp.minimum(block(c, m, j * R + rr), B - 1)
        return pltpu.make_async_copy(tab_f.at[b], tf.at[slot, :, rr * LANES:(rr + 1) * LANES], t_s.at[slot, rr])

    def table_wait(slot, rr):
        return pltpu.make_async_copy(tab_f.at[0], tf.at[slot, :, rr * LANES:(rr + 1) * LANES], t_s.at[slot, rr])

    consts = [pltpu.make_async_copy(s, d, k_s.at[k]) for k, (s, d) in enumerate(
        [(eig_r, er), (eig_c, ec), (tab_h, th), (tab_t, tt), (tab_b.at[j], tb),
         (levels_in, levels), (weights_in, weights)])]
    first_last = (M - 1) * D * LANES
    ending = pltpu.make_async_copy(tab_b.at[j, pl.ds(first_last, B * LANES - first_last)], table_out, k_s.at[8])
    fast = min(FAST, S) if half > 1 else 0
    ahead = fast * hs
    if fast:
        early = pltpu.make_async_copy(tab_p.at[r, pl.ds(0, ahead)], tp, k_s.at[7])

    load(0).start()
    for k in range(5, 7):
        consts[k].start()
    for rr in range(R):
        load_table(0, rr).start()
    for k in range(2):
        consts[k].start()
    if fast:
        early.start()

    for k in range(5, 7):
        consts[k].wait()
    tile_rows, tile_cols = rows // levels.shape[1], cols // levels.shape[2]
    tile_of = lax.broadcasted_iota(jnp.int32, (1, cols), 1) // tile_cols
    for a in range(levels.shape[1]):
        line = jnp.zeros((1, cols), jnp.float32)
        for b in range(levels.shape[2]):
            line = jnp.where(tile_of == b, levels[0, a, b].astype(jnp.float32) * 0.25, line)
        grid[a * tile_rows:(a + 1) * tile_rows, :] = jnp.broadcast_to(line, (tile_rows, cols))

    stiff = [jnp.full((1, LANES), weights[k].astype(jnp.float32)) * (1.0 / 256.0) for k in range(n)]
    couple = [2.0 * stiff[k] * stiff[k + 1] / (stiff[k] + stiff[k + 1]) for k in range(n - 1)]
    zero = jnp.zeros((1, LANES), jnp.float32)
    ends, flipped = [zero] + couple, [zero] + couple[::-1]
    own = [jnp.where(left, a, b) for a, b in zip(ends, flipped)]
    other = [jnp.where(left, b, a) for a, b in zip(ends, flipped)]
    below, above = own[0], own[1]
    for k in range(1, half):
        below = jnp.where(p == k, own[k], below)
        above = jnp.where(p == k, own[k + 1], above)

    def blend(c):
        load(c).wait()
        x[c] = (raw[c].astype(jnp.float32) * grid[...]).astype(jnp.bfloat16)

    def build_pivots(c, m, slot):
        b = jnp.minimum(block(c, m, me), B - 1)
        a = er[...] + ec[b]

        def sweep(chain):
            rest, first = None, None
            for k in range(half):
                base = a if k == 0 else a + chain[k] * rest
                inverse = 1.0 / (base + chain[k + 1])
                first = inverse if k == 0 else jnp.where(p == k, inverse, first)
                rest = base * inverse
            return base, rest, first

        base, _, first = sweep(own)
        _, rest_other, _ = sweep(other)
        dd[slot] = first
        ee[slot] = jnp.where(p == half - 1, 1.0 / (base + own[half] * rest_other), first)

    def remote(src, dst, ss, rs_, where):
        return pltpu.make_async_remote_copy(
            src_ref=src, dst_ref=dst, send_sem=ss, recv_sem=rs_,
            device_id=where, device_id_type=MESH)

    def lanes_of(c, m, d):
        return pl.ds(pl.multiple_of(jnp.minimum(block(c, m, d), B - 1) * LANES, LANES), LANES)

    def q_of(k):
        return pl.ds(pl.multiple_of(k * hs, 16), hs)

    def gather(c, d):
        return remote(x.at[c], xg.at[c, d - 1], g_s.at[c, d - 1], g_r.at[c, d - 1],
                      {"col": lax.rem(j + d, J)})

    def row_out(i, d):
        peer = lax.rem(r + d, R)
        return remote(sw.at[i, peer], fr.at[i, r], f_s.at[i, d - 1], f_r.at[i, d - 1], {"row": peer})

    def y_inner(i, k):
        return remote(yb.at[i, q_of(k)], yin.at[i, q_of(k)], y_s.at[i], y_r.at[i * S + k], {"tm": inner})

    def y_early(d, k):
        peer = lax.rem(r + d, R)
        return remote(ys.at[peer, q_of(k)], yd.at[d, q_of(k)], e_s.at[d, k], e_r.at[d, k],
                      {"tm": inner, "row": peer})

    def y_middle(i, k):
        return remote(yb.at[i, q_of(k)], zin.at[i, q_of(k)], y_s.at[i], z_r.at[i * S + k], {"tm": inner})

    def x_outer(i, k):
        return remote(xb.at[i, q_of(k)], zin.at[i, q_of(k)], x_s.at[i], z_r.at[i * S + k], {"tm": outer})

    def row_back(i, c, m, d):
        peer = lax.rem(r + d, R)
        return remote(rs.at[i, peer], rg.at[c, :, lanes_of(c, m, me)], b_s.at[i, d - 1],
                      b_r.at[i, d - 1], {"row": peer})

    def col_share(i, c, m, d, e):
        part = rg.at[c, :, lanes_of(c, m, j * R + lax.rem(r + R - d, R))]
        return remote(part, part, c_s.at[i, d, e - 1], c_r.at[i, d, e - 1],
                      {"col": lax.rem(j + e, J)})

    def whole_wait(ref, sem):
        pltpu.make_async_copy(ref, ref, sem).wait()

    def dot(a, b):
        return jnp.dot(a, b, preferred_element_type=jnp.float32)

    blend(0)

    @pl.when(p > 0)
    def _():
        pl.semaphore_wait(barrier, J + R + 2 * (R - 1))

    @pl.when(p == 0)
    def _():
        pl.semaphore_wait(barrier, J + R - 1 + R - 1)

    for d in range(1, J):
        gather(0, d).start()
    for c in range(1, C):
        load(c).start()
    for slot in range(1, len(slots)):
        for rr in range(R):
            load_table(slot, rr).start()
        if slot == 1:
            consts[2].start()
    for k in range(3, 5):
        consts[k].start()
    ending.start()
    for k in range(2):
        consts[k].wait()
    build_pivots(0, 0, 0 if M > 1 else M - 1)

    total = N * S

    def step(s, carry):
        at_u = s - LAG_U - jnp.maximum(HOP_UP * p - 1, 0)
        at_y = s - LAG_U - 1 - HOP_UP * p
        at_x = s - LAG_U - 1 - HOP_UP * (half - 1) - HOP_MID - HOP_DOWN * (half - 1 - p)
        at_w = at_x - LAG_W
        at_g = at_w - LAG_G

        @pl.when((at_x >= 0) & (at_x < total))
        def _():
            i, k = at_x // S, at_x % S
            c, m = i // M, i % M
            slot = slot_of(c, m)
            q = q_of(k)

            @pl.when(valid(c, m, me))
            def _():
                x_outer(i, k).wait_recv()
                xb[i, q] = ((u[i, q] + above * zin[i, q].astype(jnp.float32)) * ee[slot, q]).astype(jnp.bfloat16)

                @pl.when(p > 0)
                def _():
                    x_outer(i, k).start()

                @pl.when(k == S - 1)
                def _():
                    @pl.when(i == 0)
                    def _():
                        consts[3].wait()
                    for d in range(1, R):
                        peer = lax.rem(r + d, R)
                        rs[i, peer] = dot(tt[peer], xb[i]).astype(jnp.bfloat16)
                        row_back(i, c, m, d).start()
                    rg[c, :, lanes_of(c, m, me)] = dot(tt[r], xb[i]).astype(jnp.bfloat16)
                    for e in range(1, J):
                        col_share(i, c, m, 0, e).start()

        @pl.when((at_y >= 0) & (at_y < total))
        def _():
            i, k = at_y // S, at_y % S
            c, m = i // M, i % M
            slot = slot_of(c, m)
            q = q_of(k)

            is_early = (i == 0) & (k < fast)

            @pl.when(valid(c, m, me) & jnp.logical_not(is_early & (p == 0)))
            def _():
                @pl.when((p > 0) & jnp.logical_not(is_early & (p == 1)))
                def _():
                    y_inner(i, k).wait_recv()
                    u[i, q] = u[i, q] + below * yin[i, q].astype(jnp.float32)

                if fast:
                    @pl.when(is_early & (p == 1))
                    def _():
                        whole = jnp.zeros((hs, LANES), jnp.float32)
                        for d in range(R):
                            y_early(d, k).wait_recv()
                            whole += yd[d, q].astype(jnp.float32)
                        u[i, q] = u[i, q] + below * whole
                yb[i, q] = (u[i, q] * dd[slot, q]).astype(jnp.bfloat16)

                @pl.when(mid)
                def _():
                    y_middle(i, k).start()

                @pl.when(jnp.logical_not(mid))
                def _():
                    y_inner(i, k).start()

        @pl.when((at_u >= 0) & (at_u < total) & (at_u % S == 0))
        def _():
            i = at_u // S
            c, m = i // M, i % M

            @pl.when(i == 0)
            def _():
                consts[2].wait()

            @pl.when(valid(c, m, me))
            def _():
                for d in range(1, R):
                    row_out(i, d).wait_recv()
                u[i] = dot(th[...], fr[i].reshape(H, LANES))

        @pl.when((at_w >= 0) & (at_w < total) & (at_w % S == S - 1))
        def _():
            i = at_w // S
            c, m = i // M, i % M
            for d in range(1, R):
                @pl.when(valid(c, m, j * R + lax.rem(r + R - d, R)))
                def _():
                    row_back(i, c, m, d).wait_recv()
                    for e in range(1, J):
                        col_share(i, c, m, d, e).start()

        @pl.when((s < N * STRIDE) & (s % STRIDE == 0))
        def _():
            i = s // STRIDE
            c, m = i // M, i % M
            slot = slot_of(c, m)
            fresh = (c == 0) | (m == M - 1)

            @pl.when(fresh)
            def _():
                for rr in range(R):
                    table_wait(slot, rr).wait()

            def cols_of(d):
                return pl.ds(pl.multiple_of(lax.rem(j + J - d, J) * cols, 16), cols)
            first = dot(x[c], tf[slot, cols_of(0)])

            @pl.when(m == 0)
            def _():
                for d in range(1, J):
                    gather(c, d).wait_recv()
            acc = first
            for d in range(1, J):
                acc += dot(xg[c, d - 1], tf[slot, cols_of(d)])
            low = acc.astype(jnp.bfloat16)
            for rr in range(R):
                sw[i, rr] = low[:, rr * LANES:(rr + 1) * LANES]
            for d in range(1, R):
                @pl.when(valid(c, m, j * R + lax.rem(r + d, R)))
                def _():
                    row_out(i, d).start()
            fr[i, r] = sw[i, r]

            if fast:
                @pl.when((i == 0) & (p == 0))
                def _():
                    early.wait()
                    for d in range(R):
                        peer = lax.rem(r + d, R)
                        b = block(0, 0, j * R + peer)

                        @pl.when(b < B)
                        def _():
                            pivot = er[:ahead] + ec[jnp.minimum(b, B - 1)] + above
                            ys[peer] = (dot(tp[...], sw[0, peer]) * (1.0 / pivot)).astype(jnp.bfloat16)

                    for k in range(fast):
                        for d in range(R):
                            @pl.when(valid(0, 0, j * R + lax.rem(r + d, R)))
                            def _():
                                y_early(d, k).start()

                @pl.when((i == 0) & (p > 0))
                def _():
                    early.wait()

            for c_next in range(1, C):
                @pl.when(i == c_next - 1)
                def _():
                    blend(c_next)
                    for d in range(1, J):
                        gather(c_next, d).start()

            @pl.when(fresh & (i > 0))
            def _():
                build_pivots(c, m, slot)

        @pl.when((at_g >= 0) & (at_g < total) & (at_g % S == S - 1))
        def _():
            i = at_g // S
            c, m = i // M, i % M

            @pl.when(i == 0)
            def _():
                consts[4].wait()
                ending.wait()
            for d in range(R):
                for e in range(1, J):
                    @pl.when(valid(c, m, lax.rem(j + J - e, J) * R + lax.rem(r + R - d, R)))
                    def _():
                        col_share(i, c, m, d, e).wait_recv()

            if M > 1:
                @pl.when(m < M - 1)
                def _():
                    span = pl.ds(pl.multiple_of(m * D * LANES, LANES), D * LANES)
                    part = dot(rg[c, :, span], tb[span, :])

                    @pl.when(m == 0)
                    def _():
                        out[c] = part

                    @pl.when(m > 0)
                    def _():
                        out[c] = out[c] + part

            @pl.when((m == M - 1) & (i < N - 1))
            def _():
                part = dot(rg[c, :, first_last:], tb[first_last:, :])
                out[c] = part if M == 1 else out[c] + part

            @pl.when(i == N - 1)
            def _():
                back_out[...] = rg[C - 1, :, first_last:]

            for d in range(1, R):
                @pl.when(valid(c, m, j * R + lax.rem(r + d, R)))
                def _():
                    row_out(i, d).wait_send()

                @pl.when(valid(c, m, j * R + lax.rem(r + R - d, R)))
                def _():
                    for e in range(1, J):
                        col_share(i, c, m, d, e).wait_send()

            @pl.when(valid(c, m, me))
            def _():
                for d in range(1, R):
                    row_back(i, c, m, d).wait_send()
                for e in range(1, J):
                    col_share(i, c, m, 0, e).wait_send()
                @pl.when((i > 0) | (p > 0))
                def _():
                    whole_wait(yb.at[i], y_s.at[i])

                @pl.when((i == 0) & (p == 0))
                def _():
                    if fast < S:
                        whole_wait(yb.at[0, pl.ds(ahead, H - ahead)], y_s.at[0])

                @pl.when(p > 0)
                def _():
                    whole_wait(xb.at[i], x_s.at[i])
        return carry

    lax.fori_loop(0, total + LAG_U + 1 + (HOP_UP + HOP_DOWN) * (half - 1) + HOP_MID + LAG_W + LAG_G, step, 0)
    for c in range(C):
        for d in range(1, J):
            gather(c, d).wait_send()

    @pl.when(p == 0)
    def _():
        for d in range(R):
            @pl.when(valid(0, 0, j * R + lax.rem(r + d, R)))
            def _():
                for k in range(fast):
                    y_early(d, k).wait_send()


def finish(M, pieces, held, back, table, out, total, sems):
    C, rows, _ = held.shape
    copies = [pltpu.make_async_copy(held.at[c], out.at[c], sems.at[c]) for c in range(C - 1)]
    for copy in copies:
        copy.start()
    each = rows // pieces
    for a in range(pieces):
        at = pl.ds(a * each, each)
        part = jnp.dot(back[at, :], table[...], preferred_element_type=jnp.float32)
        total[at, :] = part if M == 1 else held[C - 1, at, :] + part
        copy = pltpu.make_async_copy(total.at[at], out.at[C - 1, at], sems.at[C - 1 + a])
        copy.start()
        copies.append(copy)
    for copy in copies:
        copy.wait()


def local(seams, levels, weights):
    _, C, rows, cols = seams.shape
    R, J, n = lax.axis_size("row"), lax.axis_size("col"), lax.axis_size("tm")
    H, W = rows * R, cols * J
    D = J * R
    B = W // LANES
    M = -(-B // D)
    N = C * M
    S = PARTS
    Q = M - 1 + C

    table_w, table_h = cosine_table(W), cosine_table(H)
    tab_f = jnp.asarray(np.ascontiguousarray(table_w.reshape(B, LANES, W).transpose(0, 2, 1)))
    tab_b = jnp.asarray(np.ascontiguousarray(table_w.reshape(W, J, cols).transpose(1, 0, 2)))
    tab_h = jnp.asarray(table_h)
    tab_t = jnp.asarray(np.ascontiguousarray(table_h.T).reshape(R, rows, H))
    tab_p = jnp.asarray(np.ascontiguousarray(table_h.reshape(H, R, rows).transpose(1, 0, 2)))
    eig_r = jnp.asarray(np.ascontiguousarray(
        np.broadcast_to((np.float32(screen) + laplace_eigen(H))[:, None], (H, LANES))))
    eig_c = jnp.asarray(laplace_eigen(W).reshape(B, 1, LANES))

    bf, f32 = jnp.bfloat16, jnp.float32
    tail = W - (M - 1) * D * LANES
    pieces = 2 if rows % 32 == 0 else 1
    vm, dma = pltpu.VMEM, pltpu.SemaphoreType.DMA
    hbm = pl.BlockSpec(memory_space=pltpu.HBM)
    results = pl.pallas_call(
        functools.partial(kernel, J, R, n, C, M, B, S),
        out_shape=(pltpu.VMEM((C, rows, cols), f32), pltpu.VMEM((rows, tail), bf), pltpu.VMEM((tail, cols), bf)),
        in_specs=[hbm] * 10,
        out_specs=[pl.BlockSpec(memory_space=pltpu.VMEM)] * 3,
        scratch_shapes=[
            pltpu.SMEM(levels.shape, jnp.int32),
            pltpu.SMEM(weights.shape, jnp.int32),
            vm((C, rows, cols), bf),
            vm((rows, cols), f32),
            vm((Q, W, R * LANES), bf),
            vm((W, cols), bf),
            vm((H, H), bf),
            vm((R, rows, H), bf),
            vm((max(FAST, 1) * (H // S), rows), bf),
            vm((R, max(FAST, 1) * (H // S), LANES), bf),
            vm((R, max(FAST, 1) * (H // S), LANES), bf),
            vm((H, LANES), f32),
            vm((B, 1, LANES), f32),
            vm((C, rows, cols), bf),
            vm((C, J - 1, rows, cols), bf),
            vm((N, R, rows, LANES), bf),
            vm((N, R, rows, LANES), bf),
            vm((Q, H, LANES), f32),
            vm((Q, H, LANES), f32),
            vm((N, H, LANES), f32),
            vm((N, H, LANES), bf),
            vm((N, H, LANES), bf),
            vm((N, H, LANES), bf),
            vm((N, H, LANES), bf),
            vm((N, R, rows, LANES), bf),
            vm((C, rows, W), bf),
            dma((C,)), dma((Q, R)), dma((9,)),
            dma((C, J - 1)), dma((C, J - 1)),
            dma((N, R - 1)), dma((N, R - 1)),
            dma((N,)), dma((N * S,)), dma((N * S,)), dma((N,)),
            dma((N, R - 1)), dma((N, R - 1)),
            dma((N, R, J - 1)), dma((N, R, J - 1)),
            dma((R, max(FAST, 1))), dma((R, max(FAST, 1))),
        ],
        compiler_params=pltpu.CompilerParams(
            collective_id=0, has_side_effects=True, vmem_limit_bytes=52 * 1024 * 1024),
    )(seams[0], levels, weights, tab_f, tab_b, tab_h, tab_t, tab_p, eig_r, eig_c)
    held = [pltpu.with_memory_space_constraint(v, pltpu.VMEM) for v in results]
    return pl.pallas_call(
        functools.partial(finish, M, pieces),
        out_shape=jax.ShapeDtypeStruct((C, rows, cols), f32),
        in_specs=[pl.BlockSpec(memory_space=pltpu.VMEM)] * 3,
        out_specs=hbm,
        scratch_shapes=[vm((rows, cols), f32), dma((C - 1 + pieces,))],
        compiler_params=pltpu.CompilerParams(vmem_limit_bytes=6 * 1024 * 1024),
    )(*held)[None]


def solution(mesh):
    placed = (P(("win", "tm"), None, "row", "col"), P(("win", "tm"), "row", "col"), P("win"))
    return jax.shard_map(
        local,
        mesh=mesh,
        in_specs=placed,
        out_specs=P(("win", "tm"), None, "row", "col"),
        check_vma=False,
    )
```
